32 devices in a mesh: samp: 4 (over y, x), var: 8 (over z, core).
Axes of the slice: x: 2, y: 2, z: 4, core: 2. Of those that a mesh axis runs over, the one named last changes fastest.
Arguments:
- dosage: bfloat16 [8192, 16384], P('samp', 'var'), may hold values from -6 to 6
- traits: float32 [8192, 128], P(('samp', 'var')), may hold values from -6 to 6
- coef_now: float32 [128, 256, 128], P('var', 'samp'), may hold values from -6 to 6
- coef_prev: float32 [128, 256, 128], P('var', 'samp'), may hold values from -6 to 6
- block_inverse: bfloat16 [128, 256, 4, 256], P('var', 'samp'), may hold values from -0.1875 to 0.1875
- penalty: float32 [128], replicated, may hold values from 0.05 to 0.5
- block_start: int32 [64], replicated, may hold values from 0 to 1, as said below
- unit_owner: int32 [64], replicated, may hold values from 0 to 7, as said below
Outputs:
- coef_next: float32 [128, 256, 128], P('var', 'samp')
- residual: float32 [8192, 128], P(('samp', 'var'))
The draws below stay inside these ranges and needn't reach their ends.
Inputs may be any that keep to these rules, and one draw needn't show every extreme that they name: `block_start`: 1 where a linkage block begins, else 0. The first unit of every device's 8 units begins a block, and a block holds 1 to 4 units of 256 variants. `unit_owner`: the index along var of the device that owns each unit's block, equal for all units of a block. For a unit of the device with index d along var it is (d + j) modulo the size of var, with 1 <= j <= 4. An owner holds at most 16 units and some owner holds exactly 16; the units of one device that belong to one owner are at most 4, and some device has exactly 4 for one owner.
All inputs are finite; a program needn't handle non-finite values.
Results may differ from the reference program's by a relative error of at most 0.0072.
Values may be sent and summed in bfloat16 or wider, within the bound.
No kernel may reach another device: no remote copies, remote signals or barrier semaphores. Data moves between devices by JAX's collectives and lax.ppermute only.
A program may use at most 64 MiB of HBM per device.

```python
import math
import jax
import jax.numpy as jnp
from jax import lax

K = 128
UNIT = 256
BMAX = 4
REACH = 4
NS = 8192
NV = 16384
UNITS_DEV = 8
UNITS = 64
PAIR = 4
CAP = 16
SLOTS = 128
N_VAR = 8


def layout(key):
    base = jax.random.fold_in(key, 9173)
    key_len, key_owner, key_score = jax.random.split(base, 3)
    shard_count = N_VAR
    per_shard = UNITS_DEV
    reach = REACH
    shard_ids = jnp.arange(shard_count, dtype=jnp.int32)
    hot_owner = jax.random.randint(key_owner, (), 0, shard_count)
    hot_gap = (hot_owner - shard_ids) % shard_count
    hot_shard = (hot_gap >= 1) & (hot_gap <= reach)
    lengths = jax.random.randint(key_len, (shard_count, per_shard), 1, PAIR + 1)
    lengths = lengths.at[:, 0].set(jnp.where(hot_shard, PAIR, lengths[:, 0]))
    block_ends = jnp.cumsum(lengths, axis=1)
    begins = block_ends - lengths
    positions = jnp.arange(per_shard, dtype=jnp.int32)
    starts_flag = jnp.any(begins[:, :, None] == positions[None, None, :], axis=1)
    begin_at = lax.cummax(jnp.where(starts_flag, positions[None, :], 0), axis=1)
    block_later = lax.cummin(jnp.where(starts_flag, positions[None, :], per_shard), axis=1, reverse=True)
    block_follow = jnp.concatenate([block_later[:, 1:], jnp.full((shard_count, 1), per_shard, jnp.int32)], axis=1)
    block_len = block_follow - begin_at

    def visit_unit(carried, column):
        group_fill, group_index = carried
        flag_now, length_now = column
        fresh_group = flag_now & (group_fill + length_now > PAIR)
        group_index = jnp.where(fresh_group, group_index + 1, group_index)
        group_fill = jnp.where(flag_now, jnp.where(fresh_group, length_now, group_fill + length_now), group_fill)
        return ((group_fill, group_index), group_index)
    start_state = (jnp.full((shard_count,), PAIR, jnp.int32), jnp.full((shard_count,), -1, jnp.int32))
    final_state, groups = lax.scan(visit_unit, start_state, (starts_flag.T, block_len.T))
    groups = groups.T
    reach_ids = jnp.arange(reach, dtype=jnp.int32)
    scores = jax.random.randint(key_score, (shard_count, reach), 0, 1024) * reach + reach_ids[None, :]
    forced = hot_shard[:, None] & (reach_ids[None, :] + 1 == hot_gap[:, None])
    scores = jnp.where(forced, -1, scores)
    order = jnp.argsort(scores, axis=1, stable=True).astype(jnp.int32)
    group_pick = jnp.clip(groups, 0, reach - 1)
    gaps = jnp.take_along_axis(order, group_pick, axis=1) + 1
    owners_out = ((shard_ids[:, None] + gaps) % shard_count).reshape(-1).astype(jnp.int32)
    return (starts_flag.astype(jnp.int32).reshape(-1), owners_out)


def draw_block_start(key, part):
    return layout(key)[0]


def draw_unit_owner(key, part):
    return layout(key)[1]


def strengthened(values, key, source, target, shards_of, factor):
    owner, partner = [(jnp.arange(values.shape[position]) // (values.shape[position] // shards_of)).reshape([-1 if axis == position else 1 for axis in range(values.ndim)]) for position in (source, target)]
    chosen = jax.random.permutation(key, shards_of)[partner]
    strong = (owner == chosen) | (owner == (partner + shards_of // 2) % shards_of)
    return jnp.where(strong, factor * values, values)


def block_levels(stream_key, extent, shards, low, top_value):
    factor_of = 1.0
    for axis_at, blocks in shards:
        heights = jax.random.uniform(jax.random.fold_in(jax.random.fold_in(stream_key, 6), axis_at), (blocks,), jnp.float32, low / len(shards), top_value / len(shards))
        factor_of = factor_of * jnp.repeat(jnp.exp(heights), extent[axis_at] // blocks).reshape((-1,) + (1,) * (len(extent) - 1 - axis_at))
    return factor_of


def noise(rng, dims, deviation, most, pieces=(), kind=jnp.bfloat16):
    array = jax.random.normal(rng, dims, jnp.float32) * deviation
    if len(pieces) > 0:
        array = block_levels(rng, dims, pieces, -0.22, 0.18) * array
    return jnp.clip(array, min=-most, max=most).astype(kind)


def noise_with(rng, extent, scale, most, shards, heavy, kind=jnp.bfloat16):
    drawn = scale * jax.random.normal(rng, extent, jnp.float32)
    if shards:
        drawn = drawn * block_levels(rng, extent, shards, -0.22, 0.18)
    return jnp.clip(strengthened(drawn, jax.random.fold_in(rng, 3), *heavy), -most, most).astype(kind)


def setup_inputs(seed: int = 0) -> dict:
    keys = jax.random.split(jax.random.key(seed), 9)
    dosage = noise_with(keys[0], (NS, NV), 1.0, 6.0, ((0, 4), (1, 8)), (1, 0, 8, 2.0))
    traits = noise(keys[1], (NS, K), 1.0, 6.0, ((0, 32),), jnp.float32)
    coef_now = noise(keys[2], (SLOTS, UNIT, K), 1.0, 6.0, ((0, 8), (1, 4)), jnp.float32)
    coef_prev = noise(keys[3], (SLOTS, UNIT, K), 1.0, 6.0, ((0, 8), (1, 4)), jnp.float32)
    block_inverse = noise(keys[4], (SLOTS, UNIT, BMAX, UNIT), (BMAX * UNIT) ** -0.5, 0.1875, ((0, 8), (1, 4)))
    penalty = jnp.clip(jnp.exp(jax.random.uniform(keys[5], (K,), jnp.float32, math.log(0.05), math.log(0.5))), 0.05, 0.5)
    block_start = draw_block_start(jax.random.fold_in(keys[8], 71), 0)
    unit_owner = draw_unit_owner(jax.random.fold_in(keys[8], 71), 0)
    return dict(dosage=dosage, traits=traits, coef_now=coef_now, coef_prev=coef_prev, block_inverse=block_inverse, penalty=penalty, block_start=block_start, unit_owner=unit_owner)


MOMENTA = (0.4, 0.55)

def unit_tables(block_start, unit_owner, per_device, owners):
    unit_count = block_start.shape[0]
    unit_ids = jnp.arange(unit_count, dtype=jnp.int32)
    shard_of = unit_ids // per_device
    owner_hot = (unit_owner[:, None] == jnp.arange(owners, dtype=jnp.int32)[None, :]).astype(jnp.int32)
    running = jnp.cumsum(owner_hot, axis=0) - owner_hot
    slot_index = lax.optimization_barrier(jnp.sum(running * owner_hot, axis=1))
    first_unit = shard_of * per_device
    before_shard = lax.optimization_barrier(jnp.sum(running[first_unit] * owner_hot, axis=1))
    pair_place = slot_index - before_shard
    block_begin = lax.cummax(jnp.where(block_start == 1, unit_ids, 0), axis=0)
    block_later = lax.cummin(jnp.where(block_start == 1, unit_ids, unit_count), axis=0, reverse=True)
    block_follow = jnp.concatenate([block_later[1:], jnp.full((1,), unit_count, jnp.int32)])
    block_length = block_follow - block_begin
    offset = unit_ids - block_begin
    return (shard_of, slot_index, pair_place, offset, block_length)

def soft_shrink(stepped, penalty):
    return jnp.sign(stepped) * jnp.maximum(jnp.abs(stepped) - penalty, 0.0)

def reference(dosage, traits, coef_now, coef_prev, block_inverse, penalty, block_start, unit_owner):
    shard_of, slot_index, pair_place, offset, block_length = unit_tables(block_start, unit_owner, UNITS_DEV, N_VAR)
    global_slot = (unit_owner * CAP + slot_index).astype(jnp.int32)
    inv_scale = 1.0 / math.sqrt(NV)
    grad_scale = 0.5 / math.sqrt(NS)
    current, previous = (coef_now, coef_prev)
    residual = traits
    for momentum in MOMENTA:
        point = current + momentum * (current - previous)
        unit_point = point[global_slot]
        values = unit_point.reshape(NV, K).astype(jnp.bfloat16)
        predicted = jnp.dot(dosage, values, preferred_element_type=jnp.float32) * inv_scale
        residual = predicted - traits
        residual_b = residual.astype(jnp.bfloat16)
        gradient = lax.dot_general(dosage, residual_b, (((0,), (0,)), ((), ())), preferred_element_type=jnp.float32) * grad_scale
        grad_b = gradient.astype(jnp.bfloat16).reshape(UNITS, UNIT, K)

        def direction_of(unit_at):
            block_first = unit_at - offset[unit_at]
            members = jnp.clip(block_first + jnp.arange(BMAX, dtype=jnp.int32), 0, UNITS - 1)
            live_flag = jnp.arange(BMAX, dtype=jnp.int32) < block_length[unit_at]
            block_grad = jnp.where(live_flag[:, None, None], grad_b[members].astype(jnp.float32), jnp.float32(0.0))
            panel_rows = block_inverse[global_slot[unit_at]].astype(jnp.float32)
            return jnp.einsum('rqc,qck->rk', panel_rows, block_grad)
        direction = lax.map(direction_of, jnp.arange(UNITS, dtype=jnp.int32))
        updated_units = soft_shrink(unit_point - direction, penalty)
        updated = jnp.zeros((SLOTS, UNIT, K), jnp.float32).at[global_slot].set(updated_units)
        previous, current = (current, updated)
    return (current, residual)
```

```python
import math

import jax
import jax.numpy as jnp
from jax import lax
from jax.sharding import PartitionSpec as P

MOMENTA = (0.4, 0.55)
CORES = 2


def shifted(block, axis, distance):
    count = lax.axis_size(axis)
    return lax.ppermute(block, axis, [((i - distance) % count, i) for i in range(count)])


def crossed(block, axis, mask):
    count = lax.axis_size(axis)
    return lax.ppermute(block, axis, [(i, i ^ mask) for i in range(count)])


def pick(blocks, index):
    return lax.dynamic_index_in_dim(blocks, index, 0, keepdims=False)


def scatter_sum_var(partial, var_index):
    count = lax.axis_size("var")
    chips = count // CORES
    rows = partial.shape[0] // count
    core, chip = var_index % CORES, var_index // CORES
    shaped = partial.reshape(chips, CORES, rows, -1)
    kept = lax.dynamic_index_in_dim(shaped, core, 1, keepdims=False)
    given = lax.dynamic_index_in_dim(shaped, 1 - core, 1, keepdims=False)
    pair = kept + crossed(given, "var", 1)
    pieces = [
        shifted(pick(pair, (chip + step) % chips), "var", CORES * step) for step in range(1, chips)
    ]
    total = pick(pair, chip)
    for piece in pieces:
        total = total + piece
    return total


def gather_var(rows_b, var_index):
    count = lax.axis_size("var")
    chips = count // CORES
    core, chip = var_index % CORES, var_index // CORES
    pieces = [rows_b] + [shifted(rows_b, "var", CORES * step) for step in range(1, chips)]
    order = (chip - jnp.arange(chips, dtype=jnp.int32)) % chips
    mine = jnp.stack(pieces)[order]
    other = crossed(mine, "var", 1)
    both = jnp.where(core == 0, jnp.stack([mine, other], 1), jnp.stack([other, mine], 1))
    return both.reshape(count * rows_b.shape[0], -1)


def scatter_sum_samp(shaped, samp_index):
    quarters = lax.axis_size("samp")

    def part(index):
        return lax.dynamic_index_in_dim(shaped, index, 1, keepdims=False)

    pieces = [crossed(part(samp_index ^ mask), "samp", mask) for mask in range(1, quarters)]
    total = part(samp_index)
    for piece in pieces:
        total = total + piece
    return total


def gather_samp(held):
    quarters = lax.axis_size("samp")
    samp_index = lax.axis_index("samp")
    pieces = jnp.stack([held] + [crossed(held, "samp", mask) for mask in range(1, quarters)], 1)
    order = samp_index ^ jnp.arange(quarters, dtype=jnp.int32)
    return pieces[:, order].reshape(held.shape[0], -1, held.shape[2])


def shards(dosage, traits, coef_now, coef_prev, block_inverse, penalty, block_start, unit_owner):
    owners = lax.axis_size("var")
    quarters = lax.axis_size("samp")
    var_index = lax.axis_index("var")
    samp_index = lax.axis_index("samp")
    capacity, quarter_rows, right_cols = coef_now.shape
    block_most, unit_rows = block_inverse.shape[2:]
    per_device = dosage.shape[1] // unit_rows
    pair_cap = min(block_most, per_device)
    reach = capacity // pair_cap
    codes = reach * pair_cap
    unit_count = block_start.shape[0]
    inv_scale = 1.0 / math.sqrt(dosage.shape[1] * owners)
    grad_scale = 0.5 / math.sqrt(dosage.shape[0] * quarters)

    ids = jnp.arange(unit_count, dtype=jnp.int32)
    device_of = ids // per_device
    earlier = ids[None, :] < ids[:, None]
    same_owner = earlier & (unit_owner[None, :] == unit_owner[:, None])
    slot_index = jnp.sum(same_owner.astype(jnp.int32), axis=1)
    place = jnp.sum((same_owner & (device_of[None, :] == device_of[:, None])).astype(jnp.int32), axis=1)
    starts = (ids[None, :] <= ids[:, None]) & (block_start[None, :] == 1)
    begin = jnp.max(jnp.where(starts, ids[None, :], 0), axis=1)
    later = (ids[None, :] > ids[:, None]) & (block_start[None, :] == 1)
    follow = jnp.min(jnp.where(later, ids[None, :], unit_count), axis=1)
    gap = (unit_owner - device_of) % owners
    unit_code = (gap - 1) * pair_cap + place

    code_ids = jnp.arange(codes, dtype=jnp.int32)
    owned = (unit_owner == var_index)[None, :] & (unit_code[None, :] == code_ids[:, None])
    code_live = jnp.any(owned, axis=1)
    owned = owned.astype(jnp.int32)
    code_slot = jnp.sum(owned * slot_index[None, :], axis=1)
    code_first = jnp.sum(owned * (place - ids + begin)[None, :], axis=1)
    code_length = jnp.sum(owned * (follow - begin)[None, :], axis=1)
    slot_match = code_live[None, :] & (code_slot[None, :] == jnp.arange(capacity, dtype=jnp.int32)[:, None])
    slot_live = jnp.any(slot_match, axis=1)
    slot_code = jnp.sum(slot_match.astype(jnp.int32) * code_ids[None, :], axis=1)
    local_code = lax.dynamic_slice_in_dim(unit_code, var_index * per_device, per_device)
    matches = local_code[None, :] == code_ids[:, None]
    local_ids = jnp.arange(per_device, dtype=jnp.int32)
    send_unit = jnp.sum(matches.astype(jnp.int32) * local_ids[None, :], axis=1)
    send_live = jnp.any(matches, axis=1)

    live = code_live[:, None, None]
    now = jnp.where(live, coef_now[code_slot], 0.0)
    before = jnp.where(live, coef_prev[code_slot], 0.0)

    place_ids = jnp.arange(pair_cap, dtype=jnp.int32)
    member = place_ids[None, :] - code_first[:, None]
    member_live = (member >= 0) & (member < code_length[:, None]) & code_live[:, None]
    panels = block_inverse[code_slot].reshape(codes, quarter_rows, block_most, unit_rows)
    shifts = []
    for p in range(pair_cap):
        column = jnp.zeros((codes, quarter_rows, unit_rows), jnp.bfloat16)
        for q in range(block_most):
            use = member_live[:, p] & (member[:, p] == q)
            column = jnp.where(use[:, None, None], panels[:, :, q, :], column)
        shifts.append(column)
    mixing = jnp.stack(shifts, 2).reshape(reach, pair_cap * quarter_rows, pair_cap * unit_rows)

    zero_half = jnp.zeros((), jnp.bfloat16)
    current, previous = now, before
    residual = traits
    for momentum in MOMENTA:
        point = current + momentum * (current - previous)
        outgoing = point.astype(jnp.bfloat16).reshape(reach, pair_cap, quarter_rows, right_cols)
        received = jnp.stack([shifted(outgoing[g - 1], "var", -g) for g in range(1, reach + 1)])
        local_rows = received.reshape(codes, quarter_rows, right_cols)[local_code]
        values = lax.all_gather(local_rows[:, None], "samp", axis=1, tiled=True)
        values = values.reshape(per_device * unit_rows, right_cols)
        partial = jnp.dot(dosage, values, preferred_element_type=jnp.float32) * inv_scale
        residual = scatter_sum_var(partial, var_index) - traits
        residual_b = gather_var(residual.astype(jnp.bfloat16), var_index)
        gradient = lax.dot_general(
            dosage, residual_b, (((0,), (0,)), ((), ())), preferred_element_type=jnp.float32
        ) * grad_scale
        gradient = gradient.reshape(per_device, quarters, quarter_rows, right_cols)
        own = scatter_sum_samp(gradient, samp_index).astype(jnp.bfloat16)
        leaving = jnp.where(send_live[:, None, None], own[send_unit], zero_half)
        leaving = leaving.reshape(reach, pair_cap, quarter_rows, right_cols)
        held = jnp.stack([shifted(leaving[g - 1], "var", g) for g in range(1, reach + 1)])
        whole = gather_samp(held.reshape(codes, quarter_rows, right_cols))
        whole = whole.reshape(reach, pair_cap * unit_rows, right_cols)
        direction = jnp.einsum("gic,gck->gik", mixing, whole, preferred_element_type=jnp.float32)
        stepped = point - direction.reshape(codes, quarter_rows, right_cols)
        updated = jnp.sign(stepped) * jnp.maximum(jnp.abs(stepped) - penalty, 0.0)
        previous, current = current, updated
    current = jnp.where(slot_live[:, None, None], current[slot_code], jnp.float32(0.0))
    return (current, residual)


def solution(mesh):
    placed = (
        P("samp", "var"),
        P(("samp", "var"), None),
        P("var", "samp", None),
        P("var", "samp", None),
        P("var", "samp", None, None),
        P(),
        P(),
        P(),
    )
    return jax.shard_map(
        shards,
        mesh=mesh,
        in_specs=placed,
        out_specs=(P("var", "samp", None), P(("samp", "var"), None)),
        check_vma=False,
    )
```

```python
import functools
import math

import jax
import jax.numpy as jnp
from jax import lax
from jax.experimental import pallas as pl
from jax.experimental.pallas import tpu as pltpu
from jax.sharding import PartitionSpec as P


MOMENTA = (0.4, 0.55)
CORES = 2
MIB = 1 << 20
LARGE = 42


SMEM = pl.BlockSpec(memory_space=pltpu.SMEM)
VMEM = pl.BlockSpec(memory_space=pltpu.VMEM)
FAR = pl.BlockSpec(memory_space=pl.ANY)
F32, HALF = jnp.float32, jnp.bfloat16


def like(shape, dtype):
    return jax.ShapeDtypeStruct(shape, dtype)


def local(body, scalars, arrays, outs, scratch=(), limit=8, flops=0, far=0):
    single = not isinstance(outs, list)
    moved = sum(math.prod(a.shape) * a.dtype.itemsize for a in [*arrays, *([outs] if single else outs)])
    return pl.pallas_call(
        body,
        in_specs=[SMEM] * len(scalars) + [FAR] * far + [VMEM] * (len(arrays) - far),
        out_specs=VMEM if single else [VMEM] * len(outs),
        out_shape=outs,
        scratch_shapes=list(scratch),
        compiler_params=pltpu.CompilerParams(vmem_limit_bytes=limit * MIB),
        cost_estimate=pl.CostEstimate(flops=flops, bytes_accessed=moved, transcendentals=0),
    )(*scalars, *arrays)


def shifted(block, axis, distance):
    count = lax.axis_size(axis)
    return lax.ppermute(block, axis, [((i - distance) % count, i) for i in range(count)])


def crossed(block, axis, mask):
    count = lax.axis_size(axis)
    return lax.ppermute(block, axis, [(i, i ^ mask) for i in range(count)])


def held_by(group, owner):
    return group ^ (2 * (owner & 1))


def held_by_seen(rank, variant):
    return rank ^ (2 * ((variant + rank + 1) & 1))


def to_owners(block, mask):
    quarters, owners = lax.axis_size("samp"), lax.axis_size("var")
    route = [
        (s * owners + v, (s ^ mask) * owners + (v + held_by_seen(s ^ mask, v) + 1) % owners)
        for s in range(quarters)
        for v in range(owners)
    ]
    return lax.ppermute(block, ("samp", "var"), route)


def to_variants(block, mask):
    quarters, owners = lax.axis_size("samp"), lax.axis_size("var")
    route = [
        (s * owners + o, (s ^ mask) * owners + (o - held_by(s, o) - 1) % owners)
        for s in range(quarters)
        for o in range(owners)
    ]
    return lax.ppermute(block, ("samp", "var"), route)


class Layout:
    def __init__(self, codes, capacity, per_device):
        self.slot = 0
        self.live = self.slot + codes
        self.first = self.live + codes
        self.code_of_slot = self.first + codes
        self.local = self.code_of_slot + capacity
        self.unit = self.local + per_device
        self.size = self.unit + codes


def begin_body(spot, owners, reach, pair, per_device, momentum, where, start, owner, now, before, out, *refs):
    sent, (now_here, before_here, arrived) = refs[:reach], refs[reach:]
    copies = [
        pltpu.make_async_copy(now, now_here, arrived.at[0]),
        pltpu.make_async_copy(before, before_here, arrived.at[1]),
    ]
    for copy in copies:
        copy.start()
    tables_body(spot, owners, reach, pair, per_device, where, start, owner, out)
    for copy in copies:
        copy.wait()
    for g in range(reach):
        for p in range(pair):
            slot = out[spot.slot + g * pair + p]
            live = out[spot.live + g * pair + p]
            point = now_here[slot] + momentum * (now_here[slot] - before_here[slot])
            sent[g][p] = jnp.where(live == 1, point, 0.0).astype(HALF)


def tables_body(spot, owners, reach, pair, per_device, where, start, owner, out):
    var = where[0]
    for i in range(spot.size):
        empty = spot.code_of_slot <= i < spot.local or i >= spot.unit
        out[i] = jnp.int32(-1 if empty else 0)
    devices = [lax.rem(var - gap + owners, owners) for gap in range(1, reach + 1)]
    owned = [
        [(owner[d * per_device + j] == var).astype(jnp.int32) for j in range(per_device)]
        for d in devices
    ]
    counts = [functools.reduce(lambda a, b: a + b, flags) for flags in owned]
    for g in range(reach):
        place = jnp.int32(0)
        first = jnp.int32(0)
        base = jnp.int32(0)
        for h in range(reach):
            if h != g:
                base = base + jnp.where(devices[h] < devices[g], counts[h], 0)
        for j in range(per_device):
            first = jnp.where(start[devices[g] * per_device + j] == 1, place, first)

            @pl.when(owned[g][j] == 1)
            def _():
                code = g * pair + place
                out[spot.slot + code] = base + place
                out[spot.live + code] = jnp.int32(1)
                out[spot.first + code] = first
                out[spot.code_of_slot + base + place] = code

            place = place + owned[g][j]
    mine = [owner[var * per_device + j] for j in range(per_device)]
    for j in range(per_device):
        gap = lax.rem(mine[j] - var + owners, owners)
        place = jnp.int32(0)
        for i in range(j):
            place = place + (mine[i] == mine[j]).astype(jnp.int32)
        code = (gap - 1) * pair + place
        out[spot.local + j] = code
        out[spot.unit + code] = jnp.int32(j)


def states_body(spot, quarters, pair, where, table, now, before, *outs):
    for k in range(quarters):
        for p in range(pair):
            code = held_by(where[1] ^ k, where[0]) * pair + p
            slot = table[spot.slot + code]
            live = table[spot.live + code] == 1
            outs[k][0, p] = jnp.where(live, now[slot], 0.0)
            outs[k][1, p] = jnp.where(live, before[slot], 0.0)


def panels_body(spot, quarters, pair, most, where, table, panels, *outs):
    width = panels.shape[2] // most
    for k in range(quarters):
        for p in range(pair):
            row = held_by(where[1] ^ k, where[0]) * pair
            slot = table[spot.slot + row + p]
            first = table[spot.first + row + p]
            live = table[spot.live + row + p]
            for q in range(pair):
                same = (table[spot.first + row + q] == first) & (table[spot.live + row + q] == 1)
                part = jnp.clip(q - first, 0, most - 1)
                block = panels[slot, :, pl.ds(pl.multiple_of(part * width, width), width)]
                use = same & (live == 1)
                outs[k][p, :, q * width : (q + 1) * width] = jnp.where(use, block, jnp.zeros_like(block))


def local_values_body(spot, pair, turned, where, table, *refs):
    pieces, out, held = refs[:-2], refs[-2], refs[-1]
    for k, piece in enumerate(pieces):
        held[k] = piece[...]
    for u in range(out.shape[0]):
        code = table[spot.local + u]
        group = lax.div(code, pair)
        at = (held_by_seen(group, where[0]) ^ where[1]) if turned else group
        out[u] = held[at, lax.rem(code, pair)]


def place_values(quarters, where, pieces, values):
    units, quarter_rows = pieces[0].shape[:2]
    for k in range(quarters):
        for u in range(units):
            at = u * quarters * quarter_rows + (where[1] ^ k) * quarter_rows
            values[pl.ds(pl.multiple_of(at, quarter_rows), quarter_rows), :] = pieces[k][u]


def predict_blocks(scale, blocks, values, out, ready=None):
    chips, rows = out.shape[:2]
    for i in range(chips):
        if ready is not None:
            ready[i].wait()
        block = blocks[i * rows : (i + 1) * rows, :]
        out[i] = jnp.dot(block, values[...], preferred_element_type=F32) * scale


def first_predict_body(quarters, scale, other, where, dosage, *refs):
    pieces, (out, blocks, values, arrived) = refs[:quarters], refs[quarters:]
    chips, rows = out.shape[:2]
    core, chip = lax.rem(where[0], CORES), lax.div(where[0], CORES)
    side = (1 - core) if other else core
    copies = []
    for i in range(chips):
        at = pl.multiple_of(((chip ^ i) * CORES + side) * rows, rows)
        here = blocks.at[pl.ds(i * rows, rows), :]
        copies.append(pltpu.make_async_copy(dosage.at[pl.ds(at, rows), :], here, arrived.at[i]))
        copies[-1].start()
    place_values(quarters, where, pieces, values)
    predict_blocks(scale, blocks, values, out, copies)


def predict_body(quarters, scale, where, blocks, *refs):
    pieces, (out, values) = refs[:quarters], refs[quarters:]
    place_values(quarters, where, pieces, values)
    predict_blocks(scale, blocks, values, out)


def gradient_body(quarters, units, scale, where, *refs):
    sides, pieces, outs = refs[:CORES], refs[CORES : -quarters - 2], refs[-quarters - 2 : -2]
    residual, total = refs[-2:]
    chips, rows = len(pieces) // CORES, pieces[0].shape[0]
    for i, piece in enumerate(pieces):
        residual[i * rows : (i + 1) * rows, :] = piece[...]
    turned = [residual[c * chips * rows : (c + 1) * chips * rows, :].T for c in range(CORES)]
    width = sides[0].shape[1] // units
    quarter_rows = width // quarters
    for u in range(units):
        product = jnp.dot(turned[0], sides[0][:, u * width : (u + 1) * width], preferred_element_type=F32)
        product += jnp.dot(turned[1], sides[1][:, u * width : (u + 1) * width], preferred_element_type=F32)
        total[u] = product.T * scale
        for k in range(quarters):
            at = pl.multiple_of((where[1] ^ k) * quarter_rows, quarter_rows)
            outs[k][u] = total[u, pl.ds(at, quarter_rows), :].astype(outs[k].dtype)


def leave_body(spot, quarters, pair, where, table, *refs):
    sums, outs = refs[:quarters], refs[quarters:]
    for k in range(quarters):
        for p in range(pair):
            unit = table[spot.unit + held_by_seen(where[1] ^ k, where[0]) * pair + p]
            at = jnp.maximum(unit, 0)
            total = sums[0][at]
            for j in range(1, quarters):
                total = total + sums[j][at].astype(F32)
            outs[k][p] = jnp.where(unit >= 0, total, 0.0).astype(HALF)


def update_body(quarters, momenta, where, penalty, *refs):
    last = len(momenta) == 1
    panels, pieces, states = refs[:quarters], refs[quarters : 2 * quarters], refs[2 * quarters : 3 * quarters]
    outs, gradient = refs[3 * quarters : -1], refs[-1]
    pair, quarter_rows = pieces[0].shape[:2]
    for k in range(quarters):
        for p in range(pair):
            at = p * quarters * quarter_rows + (where[1] ^ k) * quarter_rows
            gradient[pl.ds(pl.multiple_of(at, quarter_rows), quarter_rows), :] = pieces[k][p]
    for k in range(quarters):
        panel = panels[k][...].reshape(pair * quarter_rows, -1)
        direction = jnp.dot(panel, gradient[...], preferred_element_type=F32)
        direction = direction.reshape(pair, quarter_rows, -1)
        if last:
            point = states[k][...]
        else:
            now = states[k][0]
            point = now + momenta[0] * (now - states[k][1])
        stepped = point - direction
        size = jnp.maximum(jnp.abs(stepped) - penalty[...], 0.0)
        updated = jnp.where(stepped > 0, size, jnp.where(stepped < 0, -size, 0.0))
        if last:
            outs[k][...] = updated
        else:
            following = updated + momenta[1] * (updated - now)
            outs[k][...] = following
            outs[quarters + k][...] = following.astype(HALF)


def finish_body(spot, pair, where, table, *refs):
    pieces, out, held = refs[:-2], refs[-2], refs[-1]
    for k, piece in enumerate(pieces):
        held[k] = piece[...]
    for slot in range(out.shape[0]):
        code = table[spot.code_of_slot + slot]
        known = jnp.maximum(code, 0)
        block = held[held_by(lax.div(known, pair), where[0]) ^ where[1], lax.rem(known, pair)]
        out[slot] = jnp.where(code >= 0, block, 0.0)


def steps(dosage, traits, coef_now, coef_prev, block_inverse, penalty, block_start, unit_owner):
    owners = lax.axis_size("var")
    quarters = lax.axis_size("samp")
    var_index = lax.axis_index("var").astype(jnp.int32)
    samp_index = lax.axis_index("samp").astype(jnp.int32)
    capacity, quarter_rows, right_cols = coef_now.shape
    block_most, unit_rows = block_inverse.shape[2:]
    per_device = dosage.shape[1] // unit_rows
    pair = min(block_most, per_device)
    reach = capacity // pair
    assert reach == quarters and owners % CORES == 0 and owners & (owners - 1) == 0
    chips = owners // CORES
    rows = dosage.shape[0] // owners
    codes = reach * pair
    inv_scale = 1.0 / math.sqrt(dosage.shape[1] * owners)
    grad_scale = 0.5 / math.sqrt(dosage.shape[0] * quarters)
    spot = Layout(codes, capacity, per_device)
    where = jnp.stack([var_index, samp_index])
    ranks = range(quarters)
    piece = (pair, quarter_rows, right_cols)
    share = (per_device, quarter_rows, right_cols)

    table, *sent = pl.pallas_call(
        functools.partial(begin_body, spot, owners, reach, pair, per_device, MOMENTA[0]),
        name="begin",
        in_specs=[SMEM] * 3 + [FAR] * 2,
        out_specs=[SMEM] + [VMEM] * reach,
        out_shape=[like((spot.size,), jnp.int32)] + [like(piece, HALF)] * reach,
        scratch_shapes=[pltpu.VMEM(coef_now.shape, F32)] * 2 + [pltpu.SemaphoreType.DMA((2,))],
        compiler_params=pltpu.CompilerParams(vmem_limit_bytes=60 * MIB),
    )(where, block_start, unit_owner, coef_now, coef_prev)
    arrived = [shifted(sent[g], "var", -g - 1) for g in range(reach)]
    states = local(
        functools.partial(states_body, spot, quarters, pair),
        [where, table], [coef_now, coef_prev], [like((2, *piece), F32)] * quarters,
    )
    states = [states[0]] + [crossed(states[k], "samp", k) for k in ranks[1:]]
    penalty = penalty.reshape(1, 1, right_cols)

    for step in range(len(MOMENTA)):
        own = local(
            functools.partial(local_values_body, spot, pair, step > 0),
            [where, table], arrived, like(share, HALF),
            [pltpu.VMEM((reach, *piece), HALF)],
        )
        pieces = [own] + [crossed(own, "samp", k) for k in ranks[1:]]
        if step == 0:
            block_inverse = lax.optimization_barrier((own, block_inverse))[1]
            panels = local(
                functools.partial(panels_body, spot, quarters, pair, block_most),
                [where, table],
                [block_inverse.reshape(capacity, quarter_rows, block_most * unit_rows)],
                [like((pair, quarter_rows, block_most * unit_rows), HALF)] * quarters, limit=10,
            )
            pieces, panels = lax.optimization_barrier((pieces, panels))
            panels = [panels[0]] + [crossed(panels[k], "samp", k) for k in ranks[1:]]
        buffers = [pltpu.VMEM((dosage.shape[1], right_cols), HALF)]
        half = like((chips, rows, right_cols), F32)
        flops = dosage.shape[0] * dosage.shape[1] * right_cols
        if step == 0:
            block = like((chips * rows, dosage.shape[1]), HALF)
            (given, given_rows), (kept, kept_rows) = (
                local(
                    functools.partial(first_predict_body, quarters, inv_scale, other),
                    [where], [dosage, *pieces], [half, block],
                    [*buffers, pltpu.SemaphoreType.DMA((chips,))], limit=LARGE, flops=flops, far=1,
                )
                for other in (True, False)
            )
        else:
            given, kept = (
                local(
                    functools.partial(predict_body, quarters, inv_scale),
                    [where], [side, *pieces], half, buffers, limit=8, flops=flops,
                )
                for side in (given_rows, kept_rows)
            )
        both = kept + crossed(given, "var", 1)
        total = both[0]
        for i in range(1, chips):
            total = total + crossed(both[i].astype(HALF), "var", CORES * i).astype(F32)
        residual = total - traits
        residual_b = residual.astype(HALF)
        mine = [residual_b] + [crossed(residual_b, "var", CORES * i) for i in range(1, chips)]
        others = [crossed(block, "var", 1) for block in mine]
        sums = local(
            functools.partial(gradient_body, quarters, per_device, grad_scale),
            [where], [kept_rows, given_rows, *mine, *others],
            [like(share, F32 if k == 0 else HALF) for k in ranks],
            [
                pltpu.VMEM((dosage.shape[0], right_cols), HALF),
                pltpu.VMEM((per_device, unit_rows, right_cols), F32),
            ], limit=15, flops=2 * dosage.shape[0] * dosage.shape[1] * right_cols,
        )
        sums = [sums[0]] + [crossed(sums[k], "samp", k) for k in ranks[1:]]
        leaving = local(
            functools.partial(leave_body, spot, quarters, pair),
            [where, table], sums, [like(piece, HALF)] * quarters,
        )
        landed = [to_owners(leaving[k], k) for k in ranks]
        last = step == len(MOMENTA) - 1
        outs = [like(piece, F32)] * quarters + ([] if last else [like(piece, HALF)] * quarters)
        result = local(
            functools.partial(update_body, quarters, MOMENTA[step : step + 2]),
            [where], [penalty, *panels, *landed, *states], outs,
            [pltpu.VMEM((pair * unit_rows, right_cols), HALF)], limit=12,
            flops=2 * (pair * unit_rows) ** 2 * right_cols,
        )
        states = list(result[:quarters])
        if not last:
            arrived = [to_variants(result[quarters + k], k) for k in ranks]
    states = [states[0]] + [crossed(states[k], "samp", k) for k in ranks[1:]]
    current = local(
        functools.partial(finish_body, spot, pair),
        [where, table], states, like((capacity, quarter_rows, right_cols), F32),
        [pltpu.VMEM((quarters, *piece), F32)],
    )
    return (current, residual)


def solution(mesh):
    placed = (
        P("samp", "var"),
        P(("samp", "var"), None),
        P("var", "samp", None),
        P("var", "samp", None),
        P("var", "samp", None, None),
        P(),
        P(),
        P(),
    )
    return jax.shard_map(
        steps,
        mesh=mesh,
        in_specs=placed,
        out_specs=(P("var", "samp", None), P(("samp", "var"), None)),
        check_vma=False,
    )
```

```python
import functools
import math

import jax
import jax.numpy as jnp
from jax import lax
from jax.experimental import pallas as pl
from jax.experimental.pallas import tpu as pltpu
from jax.sharding import PartitionSpec as P


MOMENTA = (0.4, 0.55)
CORES = 2
MIB = 1 << 20
LARGE = 45


SMEM = pl.BlockSpec(memory_space=pltpu.SMEM)
VMEM = pl.BlockSpec(memory_space=pltpu.VMEM)
FAR = pl.BlockSpec(memory_space=pl.ANY)
F32, HALF = jnp.float32, jnp.bfloat16


def like(shape, dtype):
    return jax.ShapeDtypeStruct(shape, dtype)


def local(body, scalars, arrays, outs, scratch=(), limit=8, flops=0, far=0):
    single = not isinstance(outs, list)
    moved = sum(math.prod(a.shape) * a.dtype.itemsize for a in [*arrays, *([outs] if single else outs)])
    return pl.pallas_call(
        body,
        in_specs=[SMEM] * len(scalars) + [FAR] * far + [VMEM] * (len(arrays) - far),
        out_specs=VMEM if single else [VMEM] * len(outs),
        out_shape=outs,
        scratch_shapes=list(scratch),
        compiler_params=pltpu.CompilerParams(vmem_limit_bytes=limit * MIB),
        cost_estimate=pl.CostEstimate(flops=flops, bytes_accessed=moved, transcendentals=0),
    )(*scalars, *arrays)


def shifted(block, axis, distance):
    count = lax.axis_size(axis)
    return lax.ppermute(block, axis, [((i - distance) % count, i) for i in range(count)])


def crossed(block, axis, mask):
    count = lax.axis_size(axis)
    return lax.ppermute(block, axis, [(i, i ^ mask) for i in range(count)])


def held_by(group, owner):
    return group ^ (2 * (owner & 1))


def held_by_seen(rank, variant):
    return rank ^ (2 * ((variant + rank + 1) & 1))


def to_owners(block, mask):
    quarters, owners = lax.axis_size("samp"), lax.axis_size("var")
    route = [
        (s * owners + v, (s ^ mask) * owners + (v + held_by_seen(s ^ mask, v) + 1) % owners)
        for s in range(quarters)
        for v in range(owners)
    ]
    return lax.ppermute(block, ("samp", "var"), route)


def to_variants(block, mask):
    quarters, owners = lax.axis_size("samp"), lax.axis_size("var")
    route = [
        (s * owners + o, (s ^ mask) * owners + (o - held_by(s, o) - 1) % owners)
        for s in range(quarters)
        for o in range(owners)
    ]
    return lax.ppermute(block, ("samp", "var"), route)


class Layout:
    def __init__(self, codes, capacity, per_device):
        self.slot = 0
        self.live = self.slot + codes
        self.first = self.live + codes
        self.code_of_slot = self.first + codes
        self.local = self.code_of_slot + capacity
        self.unit = self.local + per_device
        self.size = self.unit + codes


def begin_body(spot, owners, reach, pair, per_device, momentum, where, start, owner, now, before, out, *refs):
    sent, (now_here, before_here, arrived) = refs[:reach], refs[reach:]
    copies = [
        pltpu.make_async_copy(now, now_here, arrived.at[0]),
        pltpu.make_async_copy(before, before_here, arrived.at[1]),
    ]
    for copy in copies:
        copy.start()
    tables_body(spot, owners, reach, pair, per_device, where, start, owner, out)
    for copy in copies:
        copy.wait()
    for g in range(reach):
        for p in range(pair):
            slot = out[spot.slot + g * pair + p]
            live = out[spot.live + g * pair + p]
            point = now_here[slot] + momentum * (now_here[slot] - before_here[slot])
            sent[g][p] = jnp.where(live == 1, point, 0.0).astype(HALF)


def tables_body(spot, owners, reach, pair, per_device, where, start, owner, out):
    var = where[0]
    for i in range(spot.size):
        empty = spot.code_of_slot <= i < spot.local or i >= spot.unit
        out[i] = jnp.int32(-1 if empty else 0)
    devices = [lax.rem(var - gap + owners, owners) for gap in range(1, reach + 1)]
    owned = [
        [(owner[d * per_device + j] == var).astype(jnp.int32) for j in range(per_device)]
        for d in devices
    ]
    counts = [functools.reduce(lambda a, b: a + b, flags) for flags in owned]
    for g in range(reach):
        place = jnp.int32(0)
        first = jnp.int32(0)
        base = jnp.int32(0)
        for h in range(reach):
            if h != g:
                base = base + jnp.where(devices[h] < devices[g], counts[h], 0)
        for j in range(per_device):
            first = jnp.where(start[devices[g] * per_device + j] == 1, place, first)

            @pl.when(owned[g][j] == 1)
            def _():
                code = g * pair + place
                out[spot.slot + code] = base + place
                out[spot.live + code] = jnp.int32(1)
                out[spot.first + code] = first
                out[spot.code_of_slot + base + place] = code

            place = place + owned[g][j]
    mine = [owner[var * per_device + j] for j in range(per_device)]
    for j in range(per_device):
        gap = lax.rem(mine[j] - var + owners, owners)
        place = jnp.int32(0)
        for i in range(j):
            place = place + (mine[i] == mine[j]).astype(jnp.int32)
        code = (gap - 1) * pair + place
        out[spot.local + j] = code
        out[spot.unit + code] = jnp.int32(j)


def states_body(spot, quarters, pair, where, table, now, before, *outs):
    for k in range(quarters):
        for p in range(pair):
            code = held_by(where[1] ^ k, where[0]) * pair + p
            slot = table[spot.slot + code]
            live = table[spot.live + code] == 1
            outs[k][0, p] = jnp.where(live, now[slot], 0.0)
            outs[k][1, p] = jnp.where(live, before[slot], 0.0)


def choose_body(spot, quarters, pair, where, table, inverses, *refs):
    outs, arrived = refs[:quarters], refs[quarters]
    copies = []
    for k in range(quarters):
        for p in range(pair):
            slot = table[spot.slot + held_by(where[1] ^ k, where[0]) * pair + p]
            copies.append(
                pltpu.make_async_copy(inverses.at[slot], outs[k].at[p], arrived.at[k * pair + p])
            )
            copies[-1].start()
    for copy in copies:
        copy.wait()


def panels_body(spot, quarters, pair, most, where, table, *refs):
    panels, outs = refs[:quarters], refs[quarters:]
    width = panels[0].shape[2] // most
    row = held_by(where[1], where[0]) * pair
    for p in range(pair):
        first = table[spot.first + row + p]
        live = table[spot.live + row + p] == 1
        for q in range(pair):
            same = (table[spot.first + row + q] == first) & (table[spot.live + row + q] == 1)
            part = jnp.clip(q - first, 0, most - 1)
            columns = pl.ds(pl.multiple_of(part * width, width), width)
            for k in range(quarters):
                block = panels[k][p, :, columns]
                outs[k][p, :, q * width : (q + 1) * width] = jnp.where(same & live, block, jnp.zeros_like(block))


def local_values_body(spot, pair, turned, where, table, *refs):
    pieces, out, held = refs[:-2], refs[-2], refs[-1]
    for k, piece in enumerate(pieces):
        held[k] = piece[...]
    for u in range(out.shape[0]):
        code = table[spot.local + u]
        group = lax.div(code, pair)
        at = (held_by_seen(group, where[0]) ^ where[1]) if turned else group
        out[u] = held[at, lax.rem(code, pair)]


def place_values(quarters, where, pieces, values):
    units, quarter_rows = pieces[0].shape[:2]
    for k in range(quarters):
        for u in range(units):
            at = u * quarters * quarter_rows + (where[1] ^ k) * quarter_rows
            values[pl.ds(pl.multiple_of(at, quarter_rows), quarter_rows), :] = pieces[k][u]


def load_body(where, dosage, *refs):
    outs, arrived = refs[:CORES], refs[CORES]
    core, chip = lax.rem(where[0], CORES), lax.div(where[0], CORES)
    chips = arrived.shape[0] // CORES
    rows = outs[0].shape[0] // chips
    copies = []
    for c in reversed(range(CORES)):
        for i in range(chips):
            at = pl.multiple_of(((chip ^ i) * CORES + (core ^ c)) * rows, rows)
            here = outs[c].at[pl.ds(i * rows, rows), :]
            ready = arrived.at[c * chips + i]
            copies.append(pltpu.make_async_copy(dosage.at[pl.ds(at, rows), :], here, ready))
            copies[-1].start()
    for copy in copies:
        copy.wait()


def predict_body(quarters, scale, where, blocks, *refs):
    pieces, (out, values) = refs[:quarters], refs[quarters:]
    place_values(quarters, where, pieces, values)
    chips, rows = out.shape[:2]
    for i in range(chips):
        block = blocks[i * rows : (i + 1) * rows, :]
        out[i] = jnp.dot(block, values[...], preferred_element_type=F32) * scale


def gradient_body(quarters, units, scale, where, *refs):
    sides, pieces, outs = refs[:CORES], refs[CORES : -quarters - 2], refs[-quarters - 2 : -2]
    residual, total = refs[-2:]
    chips, rows = len(pieces) // CORES, pieces[0].shape[0]
    for i, piece in enumerate(pieces):
        residual[i * rows : (i + 1) * rows, :] = piece[...]
    turned = [residual[c * chips * rows : (c + 1) * chips * rows, :].T for c in range(CORES)]
    width = sides[0].shape[1] // units
    quarter_rows = width // quarters
    for u in range(units):
        product = jnp.dot(turned[0], sides[0][:, u * width : (u + 1) * width], preferred_element_type=F32)
        product += jnp.dot(turned[1], sides[1][:, u * width : (u + 1) * width], preferred_element_type=F32)
        total[u] = product.T * scale
        for k in range(quarters):
            at = pl.multiple_of((where[1] ^ k) * quarter_rows, quarter_rows)
            outs[k][u] = total[u, pl.ds(at, quarter_rows), :].astype(outs[k].dtype)


def leave_body(spot, quarters, pair, where, table, *refs):
    sums, outs = refs[:quarters], refs[quarters:]
    for k in range(quarters):
        for p in range(pair):
            unit = table[spot.unit + held_by_seen(where[1] ^ k, where[0]) * pair + p]
            at = jnp.maximum(unit, 0)
            total = sums[0][at]
            for j in range(1, quarters):
                total = total + sums[j][at].astype(F32)
            outs[k][p] = jnp.where(unit >= 0, total, 0.0).astype(HALF)


def update_body(quarters, momenta, where, penalty, *refs):
    last = len(momenta) == 1
    panels, pieces, states = refs[:quarters], refs[quarters : 2 * quarters], refs[2 * quarters : 3 * quarters]
    outs, gradient = refs[3 * quarters : -1], refs[-1]
    pair, quarter_rows = pieces[0].shape[:2]
    for k in range(quarters):
        for p in range(pair):
            at = p * quarters * quarter_rows + (where[1] ^ k) * quarter_rows
            gradient[pl.ds(pl.multiple_of(at, quarter_rows), quarter_rows), :] = pieces[k][p]
    for k in range(quarters):
        panel = panels[k][...].reshape(pair * quarter_rows, -1)
        direction = jnp.dot(panel, gradient[...], preferred_element_type=F32)
        direction = direction.reshape(pair, quarter_rows, -1)
        if last:
            point = states[k][...]
        else:
            now = states[k][0]
            point = now + momenta[0] * (now - states[k][1])
        stepped = point - direction
        size = jnp.maximum(jnp.abs(stepped) - penalty[...], 0.0)
        updated = jnp.where(stepped > 0, size, jnp.where(stepped < 0, -size, 0.0))
        if last:
            outs[k][...] = updated
        else:
            following = updated + momenta[1] * (updated - now)
            outs[k][...] = following
            outs[quarters + k][...] = following.astype(HALF)


def finish_body(spot, pair, where, table, *refs):
    pieces, out, held = refs[:-2], refs[-2], refs[-1]
    for k, piece in enumerate(pieces):
        held[k] = piece[...]
    for slot in range(out.shape[0]):
        code = table[spot.code_of_slot + slot]
        known = jnp.maximum(code, 0)
        block = held[held_by(lax.div(known, pair), where[0]) ^ where[1], lax.rem(known, pair)]
        out[slot] = jnp.where(code >= 0, block, 0.0)


def steps(dosage, traits, coef_now, coef_prev, block_inverse, penalty, block_start, unit_owner):
    owners = lax.axis_size("var")
    quarters = lax.axis_size("samp")
    var_index = lax.axis_index("var").astype(jnp.int32)
    samp_index = lax.axis_index("samp").astype(jnp.int32)
    capacity, quarter_rows, right_cols = coef_now.shape
    block_most, unit_rows = block_inverse.shape[2:]
    per_device = dosage.shape[1] // unit_rows
    pair = min(block_most, per_device)
    reach = capacity // pair
    assert reach == quarters and owners % CORES == 0 and owners & (owners - 1) == 0
    chips = owners // CORES
    rows = dosage.shape[0] // owners
    codes = reach * pair
    inv_scale = 1.0 / math.sqrt(dosage.shape[1] * owners)
    grad_scale = 0.5 / math.sqrt(dosage.shape[0] * quarters)
    spot = Layout(codes, capacity, per_device)
    where = jnp.stack([var_index, samp_index])
    ranks = range(quarters)
    piece = (pair, quarter_rows, right_cols)
    share = (per_device, quarter_rows, right_cols)

    table, *sent = pl.pallas_call(
        functools.partial(begin_body, spot, owners, reach, pair, per_device, MOMENTA[0]),
        name="begin",
        in_specs=[SMEM] * 3 + [FAR] * 2,
        out_specs=[SMEM] + [VMEM] * reach,
        out_shape=[like((spot.size,), jnp.int32)] + [like(piece, HALF)] * reach,
        scratch_shapes=[pltpu.VMEM(coef_now.shape, F32)] * 2 + [pltpu.SemaphoreType.DMA((2,))],
        compiler_params=pltpu.CompilerParams(vmem_limit_bytes=60 * MIB),
    )(where, block_start, unit_owner, coef_now, coef_prev)
    arrived = [shifted(sent[g], "var", -g - 1) for g in range(reach)]
    states = local(
        functools.partial(states_body, spot, quarters, pair),
        [where, table], [coef_now, coef_prev], [like((2, *piece), F32)] * quarters,
    )
    chosen = local(
        functools.partial(choose_body, spot, quarters, pair),
        [where, table], [block_inverse], [like((pair, *block_inverse.shape[1:]), HALF)] * quarters,
        [pltpu.SemaphoreType.DMA((codes,))], limit=LARGE, far=1,
    )
    arrived, states, chosen = lax.optimization_barrier((arrived, states, chosen))
    states = [states[0]] + [crossed(states[k], "samp", k) for k in ranks[1:]]
    penalty = penalty.reshape(1, 1, right_cols)

    for step in range(len(MOMENTA)):
        own = local(
            functools.partial(local_values_body, spot, pair, step > 0),
            [where, table], arrived, like(share, HALF),
            [pltpu.VMEM((reach, *piece), HALF)],
        )
        pieces = [own] + [crossed(own, "samp", k) for k in ranks[1:]]
        if step == 0:
            block = like((chips * rows, dosage.shape[1]), HALF)
            dosage = lax.optimization_barrier((own, dosage))[1]
            kept_rows, given_rows = local(
                load_body, [where], [dosage], [block, block],
                [pltpu.SemaphoreType.DMA((owners,))], limit=LARGE, far=1,
            )
            pieces, kept_rows, given_rows, chosen = lax.optimization_barrier(
                (pieces, kept_rows, given_rows, chosen)
            )
            chosen = [chosen[0]] + [crossed(chosen[k], "samp", k) for k in ranks[1:]]
        buffers = [pltpu.VMEM((dosage.shape[1], right_cols), HALF)]
        half = like((chips, rows, right_cols), F32)
        flops = dosage.shape[0] * dosage.shape[1] * right_cols
        given, kept = (
            local(
                functools.partial(predict_body, quarters, inv_scale),
                [where], [side, *pieces], half, buffers, limit=8, flops=flops,
            )
            for side in (given_rows, kept_rows)
        )
        given = crossed(given, "var", 1)
        both = kept + given
        total = both[0]
        for i in range(1, chips):
            total = total + crossed(both[i].astype(HALF), "var", CORES * i).astype(F32)
        residual = total - traits
        residual_b = residual.astype(HALF)
        mine = [residual_b] + [crossed(residual_b, "var", CORES * i) for i in range(1, chips)]
        others = [crossed(block, "var", 1) for block in mine]
        sums = local(
            functools.partial(gradient_body, quarters, per_device, grad_scale),
            [where], [kept_rows, given_rows, *mine, *others],
            [like(share, F32 if k == 0 else HALF) for k in ranks],
            [
                pltpu.VMEM((dosage.shape[0], right_cols), HALF),
                pltpu.VMEM((per_device, unit_rows, right_cols), F32),
            ], limit=15, flops=2 * dosage.shape[0] * dosage.shape[1] * right_cols,
        )
        owned = sums[0]
        sums = [owned] + [crossed(sums[k], "samp", k) for k in ranks[1:]]
        if step == 0:
            chosen = lax.optimization_barrier((owned, chosen))[1]
            panels = local(
                functools.partial(panels_body, spot, quarters, pair, block_most),
                [where, table],
                [part.reshape(pair, quarter_rows, block_most * unit_rows) for part in chosen],
                [like((pair, quarter_rows, block_most * unit_rows), HALF)] * quarters, limit=10,
            )
            sums, panels = lax.optimization_barrier((sums, panels))
        leaving = local(
            functools.partial(leave_body, spot, quarters, pair),
            [where, table], sums, [like(piece, HALF)] * quarters,
        )
        landed = [to_owners(leaving[k], k) for k in ranks]
        last = step == len(MOMENTA) - 1
        outs = [like(piece, F32)] * quarters + ([] if last else [like(piece, HALF)] * quarters)
        result = local(
            functools.partial(update_body, quarters, MOMENTA[step : step + 2]),
            [where], [penalty, *panels, *landed, *states], outs,
            [pltpu.VMEM((pair * unit_rows, right_cols), HALF)], limit=12,
            flops=2 * (pair * unit_rows) ** 2 * right_cols,
        )
        states = list(result[:quarters])
        if not last:
            arrived = [to_variants(result[quarters + k], k) for k in ranks]
    states = [states[0]] + [crossed(states[k], "samp", k) for k in ranks[1:]]
    current = local(
        functools.partial(finish_body, spot, pair),
        [where, table], states, like((capacity, quarter_rows, right_cols), F32),
        [pltpu.VMEM((quarters, *piece), F32)],
    )
    return (current, residual)


def solution(mesh):
    placed = (
        P("samp", "var"),
        P(("samp", "var"), None),
        P("var", "samp", None),
        P("var", "samp", None),
        P("var", "samp", None, None),
        P(),
        P(),
        P(),
    )
    return jax.shard_map(
        steps,
        mesh=mesh,
        in_specs=placed,
        out_specs=(P("var", "samp", None), P(("samp", "var"), None)),
        check_vma=False,
    )
```

```python
import functools
import math

import jax
import jax.numpy as jnp
from jax import lax
from jax.experimental import pallas as pl
from jax.experimental.pallas import tpu as pltpu
from jax.sharding import PartitionSpec as P


MOMENTA = (0.4, 0.55)
CORES = 2
MIB = 1 << 20
LARGE = 45
LARGE_PREPARE = 57


SMEM = pl.BlockSpec(memory_space=pltpu.SMEM)
VMEM = pl.BlockSpec(memory_space=pltpu.VMEM)
FAR = pl.BlockSpec(memory_space=pl.ANY)
F32, HALF = jnp.float32, jnp.bfloat16


def like(shape, dtype):
    return jax.ShapeDtypeStruct(shape, dtype)


def local(body, scalars, arrays, outs, scratch=(), limit=8, flops=0, far=0):
    single = not isinstance(outs, list)
    moved = sum(math.prod(a.shape) * a.dtype.itemsize for a in [*arrays, *([outs] if single else outs)])
    return pl.pallas_call(
        body,
        in_specs=[SMEM] * len(scalars) + [FAR] * far + [VMEM] * (len(arrays) - far),
        out_specs=VMEM if single else [VMEM] * len(outs),
        out_shape=outs,
        scratch_shapes=list(scratch),
        compiler_params=pltpu.CompilerParams(vmem_limit_bytes=limit * MIB),
        cost_estimate=pl.CostEstimate(flops=flops, bytes_accessed=moved, transcendentals=0),
    )(*scalars, *arrays)


def indices():
    return [lax.axis_index(axis).astype(jnp.int32) for axis in ("var", "samp")]


def shifted(block, axis, distance):
    count = lax.axis_size(axis)
    return lax.ppermute(block, axis, [((i - distance) % count, i) for i in range(count)])


def crossed(block, axis, mask):
    count = lax.axis_size(axis)
    return lax.ppermute(block, axis, [(i, i ^ mask) for i in range(count)])


def held_by(group, owner):
    return group ^ (2 * (owner & 1))


def held_by_seen(rank, variant):
    return rank ^ (2 * ((variant + rank + 1) & 1))


def to_owners(block, mask):
    quarters, owners = lax.axis_size("samp"), lax.axis_size("var")
    route = [
        (s * owners + v, (s ^ mask) * owners + (v + held_by_seen(s ^ mask, v) + 1) % owners)
        for s in range(quarters)
        for v in range(owners)
    ]
    return lax.ppermute(block, ("samp", "var"), route)


def to_variants(block, mask):
    quarters, owners = lax.axis_size("samp"), lax.axis_size("var")
    route = [
        (s * owners + o, (s ^ mask) * owners + (o - held_by(s, o) - 1) % owners)
        for s in range(quarters)
        for o in range(owners)
    ]
    return lax.ppermute(block, ("samp", "var"), route)


class Layout:
    def __init__(self, codes, capacity, per_device):
        self.slot = 0
        self.live = self.slot + codes
        self.first = self.live + codes
        self.code_of_slot = self.first + codes
        self.local = self.code_of_slot + capacity
        self.unit = self.local + per_device
        self.size = self.unit + codes


def begin_body(spot, owners, reach, pair, per_device, momentum, start, owner, now, before, out, *refs):
    sent, (now_here, before_here, arrived) = refs[:reach], refs[reach:]
    copies = [
        pltpu.make_async_copy(now, now_here, arrived.at[0]),
        pltpu.make_async_copy(before, before_here, arrived.at[1]),
    ]
    for copy in copies:
        copy.start()
    tables_body(spot, owners, reach, pair, per_device, start, owner, out)
    for copy in copies:
        copy.wait()
    for g in range(reach):
        for p in range(pair):
            slot = out[spot.slot + g * pair + p]
            live = out[spot.live + g * pair + p]
            point = now_here[slot] + momentum * (now_here[slot] - before_here[slot])
            sent[g][p] = jnp.where(live == 1, point, 0.0).astype(HALF)


def tables_body(spot, owners, reach, pair, per_device, start, owner, out):
    where = indices()
    var = where[0]
    for i in range(spot.size):
        empty = spot.code_of_slot <= i < spot.local or i >= spot.unit
        out[i] = jnp.int32(-1 if empty else 0)
    devices = [lax.rem(var - gap + owners, owners) for gap in range(1, reach + 1)]
    owned = [
        [(owner[d * per_device + j] == var).astype(jnp.int32) for j in range(per_device)]
        for d in devices
    ]
    counts = [functools.reduce(lambda a, b: a + b, flags) for flags in owned]
    for g in range(reach):
        place = jnp.int32(0)
        first = jnp.int32(0)
        base = jnp.int32(0)
        for h in range(reach):
            if h != g:
                base = base + jnp.where(devices[h] < devices[g], counts[h], 0)
        for j in range(per_device):
            first = jnp.where(start[devices[g] * per_device + j] == 1, place, first)

            @pl.when(owned[g][j] == 1)
            def _():
                code = g * pair + place
                out[spot.slot + code] = base + place
                out[spot.live + code] = jnp.int32(1)
                out[spot.first + code] = first
                out[spot.code_of_slot + base + place] = code

            place = place + owned[g][j]
    mine = [owner[var * per_device + j] for j in range(per_device)]
    for j in range(per_device):
        gap = lax.rem(mine[j] - var + owners, owners)
        place = jnp.int32(0)
        for i in range(j):
            place = place + (mine[i] == mine[j]).astype(jnp.int32)
        code = (gap - 1) * pair + place
        out[spot.local + j] = code
        out[spot.unit + code] = jnp.int32(j)


def prepare_body(spot, quarters, pair, table, now, before, inverses, *refs):
    states, chosen = refs[:quarters], refs[quarters : 2 * quarters]
    now_here, before_here, arrived = refs[2 * quarters :]
    where = indices()
    copies = [
        pltpu.make_async_copy(now, now_here, arrived.at[0]),
        pltpu.make_async_copy(before, before_here, arrived.at[1]),
    ]
    for k in range(quarters):
        for p in range(pair):
            slot = table[spot.slot + held_by(where[1] ^ k, where[0]) * pair + p]
            ready = arrived.at[2 + k * pair + p]
            copies.append(pltpu.make_async_copy(inverses.at[slot], chosen[k].at[p], ready))
    for copy in copies:
        copy.start()
    for copy in copies[:2]:
        copy.wait()
    for k in range(quarters):
        for p in range(pair):
            code = held_by(where[1] ^ k, where[0]) * pair + p
            slot = table[spot.slot + code]
            live = table[spot.live + code] == 1
            states[k][0, p] = jnp.where(live, now_here[slot], 0.0)
            states[k][1, p] = jnp.where(live, before_here[slot], 0.0)
    for copy in copies[2:]:
        copy.wait()


def panels_body(spot, quarters, pair, most, table, *refs):
    where = indices()
    panels, outs = refs[:quarters], refs[quarters:]
    width = panels[0].shape[2] // most
    row = held_by(where[1], where[0]) * pair
    for p in range(pair):
        first = table[spot.first + row + p]
        live = table[spot.live + row + p] == 1
        for q in range(pair):
            same = (table[spot.first + row + q] == first) & (table[spot.live + row + q] == 1)
            part = jnp.clip(q - first, 0, most - 1)
            columns = pl.ds(pl.multiple_of(part * width, width), width)
            for k in range(quarters):
                block = panels[k][p, :, columns]
                outs[k][p, :, q * width : (q + 1) * width] = jnp.where(same & live, block, jnp.zeros_like(block))


def local_values_body(spot, pair, turned, table, *refs):
    where = indices()
    pieces, out, held = refs[:-2], refs[-2], refs[-1]
    for k, piece in enumerate(pieces):
        held[k] = piece[...]
    for u in range(out.shape[0]):
        code = table[spot.local + u]
        group = lax.div(code, pair)
        at = (held_by_seen(group, where[0]) ^ where[1]) if turned else group
        out[u] = held[at, lax.rem(code, pair)]


def place_values(quarters, where, pieces, values):
    units, quarter_rows = pieces[0].shape[:2]
    for k in range(quarters):
        for u in range(units):
            at = u * quarters * quarter_rows + (where[1] ^ k) * quarter_rows
            values[pl.ds(pl.multiple_of(at, quarter_rows), quarter_rows), :] = pieces[k][u]


def load_body(dosage, *refs):
    where = indices()
    outs, arrived = refs[:CORES], refs[CORES]
    core, chip = lax.rem(where[0], CORES), lax.div(where[0], CORES)
    chips = arrived.shape[0] // CORES
    rows = outs[0].shape[0] // chips
    copies = []
    for c in reversed(range(CORES)):
        for i in range(chips):
            at = pl.multiple_of(((chip ^ i) * CORES + (core ^ c)) * rows, rows)
            here = outs[c].at[pl.ds(i * rows, rows), :]
            ready = arrived.at[c * chips + i]
            copies.append(pltpu.make_async_copy(dosage.at[pl.ds(at, rows), :], here, ready))
            copies[-1].start()
    for copy in copies:
        copy.wait()


def predict_body(quarters, scale, blocks, *refs):
    where = indices()
    pieces, (out, values) = refs[:quarters], refs[quarters:]
    place_values(quarters, where, pieces, values)
    chips, rows = out.shape[:2]
    for i in range(chips):
        block = blocks[i * rows : (i + 1) * rows, :]
        out[i] = jnp.dot(block, values[...], preferred_element_type=F32) * scale


def gradient_body(quarters, units, scale, *refs):
    where = indices()
    sides, pieces, outs = refs[:CORES], refs[CORES : -quarters - 2], refs[-quarters - 2 : -2]
    residual, total = refs[-2:]
    chips, rows = len(pieces) // CORES, pieces[0].shape[0]
    for i, piece in enumerate(pieces):
        residual[i * rows : (i + 1) * rows, :] = piece[...]
    turned = [residual[c * chips * rows : (c + 1) * chips * rows, :].T for c in range(CORES)]
    width = sides[0].shape[1] // units
    quarter_rows = width // quarters
    for u in range(units):
        product = jnp.dot(turned[0], sides[0][:, u * width : (u + 1) * width], preferred_element_type=F32)
        product += jnp.dot(turned[1], sides[1][:, u * width : (u + 1) * width], preferred_element_type=F32)
        total[u] = product.T * scale
        for k in range(quarters):
            at = pl.multiple_of((where[1] ^ k) * quarter_rows, quarter_rows)
            outs[k][u] = total[u, pl.ds(at, quarter_rows), :].astype(outs[k].dtype)


def leave_body(spot, quarters, pair, table, *refs):
    where = indices()
    sums, outs = refs[:quarters], refs[quarters:]
    for k in range(quarters):
        for p in range(pair):
            unit = table[spot.unit + held_by_seen(where[1] ^ k, where[0]) * pair + p]
            at = jnp.maximum(unit, 0)
            total = sums[0][at]
            for j in range(1, quarters):
                total = total + sums[j][at].astype(F32)
            outs[k][p] = jnp.where(unit >= 0, total, 0.0).astype(HALF)


def update_body(quarters, momenta, penalty, *refs):
    where = indices()
    last = len(momenta) == 1
    panels, pieces, states = refs[:quarters], refs[quarters : 2 * quarters], refs[2 * quarters : 3 * quarters]
    outs, gradient = refs[3 * quarters : -1], refs[-1]
    pair, quarter_rows = pieces[0].shape[:2]
    for k in range(quarters):
        for p in range(pair):
            at = p * quarters * quarter_rows + (where[1] ^ k) * quarter_rows
            gradient[pl.ds(pl.multiple_of(at, quarter_rows), quarter_rows), :] = pieces[k][p]
    for k in range(quarters):
        panel = panels[k][...].reshape(pair * quarter_rows, -1)
        direction = jnp.dot(panel, gradient[...], preferred_element_type=F32)
        direction = direction.reshape(pair, quarter_rows, -1)
        if last:
            point = states[k][...]
        else:
            now = states[k][0]
            point = now + momenta[0] * (now - states[k][1])
        stepped = point - direction
        size = jnp.maximum(jnp.abs(stepped) - penalty[...], 0.0)
        updated = jnp.where(stepped > 0, size, jnp.where(stepped < 0, -size, 0.0))
        if last:
            outs[k][...] = updated
        else:
            following = updated + momenta[1] * (updated - now)
            outs[k][...] = following
            outs[quarters + k][...] = following.astype(HALF)


def finish_body(spot, pair, table, *refs):
    where = indices()
    pieces, out, held = refs[:-2], refs[-2], refs[-1]
    for k, piece in enumerate(pieces):
        held[k] = piece[...]
    for slot in range(out.shape[0]):
        code = table[spot.code_of_slot + slot]
        known = jnp.maximum(code, 0)
        block = held[held_by(lax.div(known, pair), where[0]) ^ where[1], lax.rem(known, pair)]
        out[slot] = jnp.where(code >= 0, block, 0.0)


def steps(dosage, traits, coef_now, coef_prev, block_inverse, penalty, block_start, unit_owner):
    owners = lax.axis_size("var")
    quarters = lax.axis_size("samp")
    capacity, quarter_rows, right_cols = coef_now.shape
    block_most, unit_rows = block_inverse.shape[2:]
    per_device = dosage.shape[1] // unit_rows
    pair = min(block_most, per_device)
    reach = capacity // pair
    assert reach == quarters and owners % CORES == 0 and owners & (owners - 1) == 0
    chips = owners // CORES
    rows = dosage.shape[0] // owners
    codes = reach * pair
    inv_scale = 1.0 / math.sqrt(dosage.shape[1] * owners)
    grad_scale = 0.5 / math.sqrt(dosage.shape[0] * quarters)
    spot = Layout(codes, capacity, per_device)
    ranks = range(quarters)
    piece = (pair, quarter_rows, right_cols)
    share = (per_device, quarter_rows, right_cols)

    table, *sent = pl.pallas_call(
        functools.partial(begin_body, spot, owners, reach, pair, per_device, MOMENTA[0]),
        name="begin",
        in_specs=[SMEM] * 2 + [FAR] * 2,
        out_specs=[SMEM] + [VMEM] * reach,
        out_shape=[like((spot.size,), jnp.int32)] + [like(piece, HALF)] * reach,
        scratch_shapes=[pltpu.VMEM(coef_now.shape, F32)] * 2 + [pltpu.SemaphoreType.DMA((2,))],
        compiler_params=pltpu.CompilerParams(vmem_limit_bytes=60 * MIB),
    )(block_start, unit_owner, coef_now, coef_prev)
    arrived = [shifted(sent[g], "var", -g - 1) for g in range(reach)]
    prepared = local(
        functools.partial(prepare_body, spot, quarters, pair),
        [table], [coef_now, coef_prev, block_inverse],
        [like((2, *piece), F32)] * quarters + [like((pair, *block_inverse.shape[1:]), HALF)] * quarters,
        [pltpu.VMEM(coef_now.shape, F32)] * 2 + [pltpu.SemaphoreType.DMA((2 + codes,))], limit=LARGE_PREPARE, far=3,
    )
    block = like((chips * rows, dosage.shape[1]), HALF)
    dosage = lax.optimization_barrier((prepared[0], dosage))[1]
    kept_rows, given_rows = local(
        load_body, [], [dosage], [block, block], [pltpu.SemaphoreType.DMA((owners,))], limit=LARGE, far=1
    )
    arrived, prepared, kept_rows, given_rows = lax.optimization_barrier(
        (arrived, prepared, kept_rows, given_rows)
    )
    states, chosen = prepared[:quarters], prepared[quarters:]
    states = [states[0]] + [crossed(states[k], "samp", k) for k in ranks[1:]]
    penalty = penalty.reshape(1, 1, right_cols)

    for step in range(len(MOMENTA)):
        own = local(
            functools.partial(local_values_body, spot, pair, step > 0),
            [table], arrived, like(share, HALF),
            [pltpu.VMEM((reach, *piece), HALF)],
        )
        pieces = [own] + [crossed(own, "samp", k) for k in ranks[1:]]
        if step == 0:
            pieces, chosen = lax.optimization_barrier((pieces, chosen))
            chosen = [chosen[0]] + [crossed(chosen[k], "samp", k) for k in ranks[1:]]
        buffers = [pltpu.VMEM((dosage.shape[1], right_cols), HALF)]
        half = like((chips, rows, right_cols), F32)
        flops = dosage.shape[0] * dosage.shape[1] * right_cols
        given, kept = (
            local(
                functools.partial(predict_body, quarters, inv_scale),
                [], [side, *pieces], half, buffers, limit=8, flops=flops,
            )
            for side in (given_rows, kept_rows)
        )
        given = crossed(given, "var", 1)
        both = kept + given
        total = both[0]
        for i in range(1, chips):
            total = total + crossed(both[i].astype(HALF), "var", CORES * i).astype(F32)
        residual_b = (total - traits).astype(HALF)
        mine = [residual_b] + [crossed(residual_b, "var", CORES * i) for i in range(1, chips)]
        others = [crossed(block, "var", 1) for block in mine]
        sums = local(
            functools.partial(gradient_body, quarters, per_device, grad_scale),
            [], [kept_rows, given_rows, *mine, *others],
            [like(share, F32 if k == 0 else HALF) for k in ranks],
            [
                pltpu.VMEM((dosage.shape[0], right_cols), HALF),
                pltpu.VMEM((per_device, unit_rows, right_cols), F32),
            ], limit=15, flops=2 * dosage.shape[0] * dosage.shape[1] * right_cols,
        )
        if step == len(MOMENTA) - 1:
            residual = lax.optimization_barrier((sums[0], total))[1] - traits
        sums = [sums[0]] + [crossed(sums[k], "samp", k) for k in ranks[1:]]
        leaving = local(
            functools.partial(leave_body, spot, quarters, pair),
            [table], sums, [like(piece, HALF)] * quarters,
        )
        landed = [to_owners(leaving[k], k) for k in ranks]
        if step == 0:
            chosen = lax.optimization_barrier((leaving, chosen))[1]
            panels = local(
                functools.partial(panels_body, spot, quarters, pair, block_most),
                [table],
                [part.reshape(pair, quarter_rows, block_most * unit_rows) for part in chosen],
                [like((pair, quarter_rows, block_most * unit_rows), HALF)] * quarters, limit=10,
            )
        last = step == len(MOMENTA) - 1
        outs = [like(piece, F32)] * quarters + ([] if last else [like(piece, HALF)] * quarters)
        result = local(
            functools.partial(update_body, quarters, MOMENTA[step : step + 2]),
            [], [penalty, *panels, *landed, *states], outs,
            [pltpu.VMEM((pair * unit_rows, right_cols), HALF)], limit=12,
            flops=2 * (pair * unit_rows) ** 2 * right_cols,
        )
        states = list(result[:quarters])
        if not last:
            arrived = [to_variants(result[quarters + k], k) for k in ranks]
    states = [states[0]] + [crossed(states[k], "samp", k) for k in ranks[1:]]
    current = local(
        functools.partial(finish_body, spot, pair),
        [table], states, like((capacity, quarter_rows, right_cols), F32),
        [pltpu.VMEM((quarters, *piece), F32)],
    )
    return (current, residual)


def solution(mesh):
    placed = (
        P("samp", "var"),
        P(("samp", "var"), None),
        P("var", "samp", None),
        P("var", "samp", None),
        P("var", "samp", None, None),
        P(),
        P(),
        P(),
    )
    return jax.shard_map(
        steps,
        mesh=mesh,
        in_specs=placed,
        out_specs=(P("var", "samp", None), P(("samp", "var"), None)),
        check_vma=False,
    )
```

```python
import functools
import math

import jax
import jax.numpy as jnp
from jax import lax
from jax.experimental import pallas as pl
from jax.experimental.pallas import tpu as pltpu
from jax.sharding import PartitionSpec as P


MOMENTA = (0.4, 0.55)
CORES = 2
MIB = 1 << 20
LARGE = 45
LARGE_PREPARE = 50


SMEM = pl.BlockSpec(memory_space=pltpu.SMEM)
VMEM = pl.BlockSpec(memory_space=pltpu.VMEM)
FAR = pl.BlockSpec(memory_space=pl.ANY)
F32, HALF = jnp.float32, jnp.bfloat16


def like(shape, dtype):
    return jax.ShapeDtypeStruct(shape, dtype)


def local(body, scalars, arrays, outs, scratch=(), limit=8, flops=0, far=0):
    single = not isinstance(outs, list)
    moved = sum(math.prod(a.shape) * a.dtype.itemsize for a in [*arrays, *([outs] if single else outs)])
    return pl.pallas_call(
        body,
        in_specs=[SMEM] * len(scalars) + [FAR] * far + [VMEM] * (len(arrays) - far),
        out_specs=VMEM if single else [VMEM] * len(outs),
        out_shape=outs,
        scratch_shapes=list(scratch),
        compiler_params=pltpu.CompilerParams(vmem_limit_bytes=limit * MIB),
        cost_estimate=pl.CostEstimate(flops=flops, bytes_accessed=moved, transcendentals=0),
    )(*scalars, *arrays)


def indices():
    return [lax.axis_index(axis).astype(jnp.int32) for axis in ("var", "samp")]


def shifted(block, axis, distance):
    count = lax.axis_size(axis)
    return lax.ppermute(block, axis, [((i - distance) % count, i) for i in range(count)])


def crossed(block, axis, mask):
    count = lax.axis_size(axis)
    return lax.ppermute(block, axis, [(i, i ^ mask) for i in range(count)])


def held_by(group, owner):
    return group ^ (2 * (owner & 1))


def held_by_seen(rank, variant):
    return rank ^ (2 * ((variant + rank + 1) & 1))


def to_owners(block, mask):
    quarters, owners = lax.axis_size("samp"), lax.axis_size("var")
    route = [
        (s * owners + v, (s ^ mask) * owners + (v + held_by_seen(s ^ mask, v) + 1) % owners)
        for s in range(quarters)
        for v in range(owners)
    ]
    return lax.ppermute(block, ("samp", "var"), route)


def to_variants(block, mask):
    quarters, owners = lax.axis_size("samp"), lax.axis_size("var")
    route = [
        (s * owners + o, (s ^ mask) * owners + (o - held_by(s, o) - 1) % owners)
        for s in range(quarters)
        for o in range(owners)
    ]
    return lax.ppermute(block, ("samp", "var"), route)


class Layout:
    def __init__(self, codes, capacity, per_device):
        self.slot = 0
        self.live = self.slot + codes
        self.first = self.live + codes
        self.code_of_slot = self.first + codes
        self.local = self.code_of_slot + capacity
        self.unit = self.local + per_device
        self.size = self.unit + codes


def begin_body(spot, owners, reach, pair, per_device, momentum, start, owner, now, before, out, *refs):
    sent, (now_here, before_here, arrived) = refs[:reach], refs[reach:]
    copies = [
        pltpu.make_async_copy(now, now_here, arrived.at[0]),
        pltpu.make_async_copy(before, before_here, arrived.at[1]),
    ]
    for copy in copies:
        copy.start()
    tables_body(spot, owners, reach, pair, per_device, start, owner, out)
    for copy in copies:
        copy.wait()
    for g in range(reach):
        for p in range(pair):
            slot = out[spot.slot + g * pair + p]
            live = out[spot.live + g * pair + p]
            point = now_here[slot] + momentum * (now_here[slot] - before_here[slot])
            sent[g][p] = jnp.where(live == 1, point, 0.0).astype(HALF)


def tables_body(spot, owners, reach, pair, per_device, start, owner, out):
    where = indices()
    var = where[0]
    for i in range(spot.size):
        empty = spot.code_of_slot <= i < spot.local or i >= spot.unit
        out[i] = jnp.int32(-1 if empty else 0)
    devices = [lax.rem(var - gap + owners, owners) for gap in range(1, reach + 1)]
    owned = [
        [(owner[d * per_device + j] == var).astype(jnp.int32) for j in range(per_device)]
        for d in devices
    ]
    counts = [functools.reduce(lambda a, b: a + b, flags) for flags in owned]
    for g in range(reach):
        place = jnp.int32(0)
        first = jnp.int32(0)
        base = jnp.int32(0)
        for h in range(reach):
            if h != g:
                base = base + jnp.where(devices[h] < devices[g], counts[h], 0)
        for j in range(per_device):
            first = jnp.where(start[devices[g] * per_device + j] == 1, place, first)

            @pl.when(owned[g][j] == 1)
            def _():
                code = g * pair + place
                out[spot.slot + code] = base + place
                out[spot.live + code] = jnp.int32(1)
                out[spot.first + code] = first
                out[spot.code_of_slot + base + place] = code

            place = place + owned[g][j]
    mine = [owner[var * per_device + j] for j in range(per_device)]
    for j in range(per_device):
        gap = lax.rem(mine[j] - var + owners, owners)
        place = jnp.int32(0)
        for i in range(j):
            place = place + (mine[i] == mine[j]).astype(jnp.int32)
        code = (gap - 1) * pair + place
        out[spot.local + j] = code
        out[spot.unit + code] = jnp.int32(j)


def prepare_body(spot, quarters, pair, table, now, before, inverses, *refs):
    states, chosen = refs[:quarters], refs[quarters : 2 * quarters]
    now_here, before_here, arrived = refs[2 * quarters :]
    where = indices()
    copies = [
        pltpu.make_async_copy(now, now_here, arrived.at[0]),
        pltpu.make_async_copy(before, before_here, arrived.at[1]),
    ]
    for k in range(quarters):
        for p in range(pair):
            slot = table[spot.slot + held_by(where[1] ^ k, where[0]) * pair + p]
            ready = arrived.at[2 + k * pair + p]
            copies.append(pltpu.make_async_copy(inverses.at[slot], chosen[k].at[p], ready))
    for copy in copies:
        copy.start()
    for copy in copies[:2]:
        copy.wait()
    for k in range(quarters):
        for p in range(pair):
            code = held_by(where[1] ^ k, where[0]) * pair + p
            slot = table[spot.slot + code]
            live = table[spot.live + code] == 1
            states[k][0, p] = jnp.where(live, now_here[slot], 0.0)
            states[k][1, p] = jnp.where(live, before_here[slot], 0.0)
    for copy in copies[2:]:
        copy.wait()


def panels_body(spot, quarters, pair, most, table, *refs):
    where = indices()
    panels, outs = refs[:quarters], refs[quarters:]
    width = panels[0].shape[2] // most
    row = held_by(where[1], where[0]) * pair
    for p in range(pair):
        first = table[spot.first + row + p]
        live = table[spot.live + row + p] == 1
        for q in range(pair):
            same = (table[spot.first + row + q] == first) & (table[spot.live + row + q] == 1)
            part = jnp.clip(q - first, 0, most - 1)
            columns = pl.ds(pl.multiple_of(part * width, width), width)
            for k in range(quarters):
                block = panels[k][p, :, columns]
                outs[k][p, :, q * width : (q + 1) * width] = jnp.where(same & live, block, jnp.zeros_like(block))


def local_values_body(spot, pair, turned, table, *refs):
    where = indices()
    pieces, out, held = refs[:-2], refs[-2], refs[-1]
    for k, piece in enumerate(pieces):
        held[k] = piece[...]
    for u in range(out.shape[0]):
        code = table[spot.local + u]
        group = lax.div(code, pair)
        at = (held_by_seen(group, where[0]) ^ where[1]) if turned else group
        out[u] = held[at, lax.rem(code, pair)]


def place_values(quarters, where, pieces, values):
    units, quarter_rows = pieces[0].shape[:2]
    for k in range(quarters):
        for u in range(units):
            at = u * quarters * quarter_rows + (where[1] ^ k) * quarter_rows
            values[pl.ds(pl.multiple_of(at, quarter_rows), quarter_rows), :] = pieces[k][u]


def load_body(dosage, *refs):
    where = indices()
    outs, arrived = refs[:CORES], refs[CORES]
    core, chip = lax.rem(where[0], CORES), lax.div(where[0], CORES)
    chips = arrived.shape[0] // CORES
    rows = outs[0].shape[0] // chips
    copies = []
    for c in reversed(range(CORES)):
        for i in range(chips):
            at = pl.multiple_of(((chip ^ i) * CORES + (core ^ c)) * rows, rows)
            here = outs[c].at[pl.ds(i * rows, rows), :]
            ready = arrived.at[c * chips + i]
            copies.append(pltpu.make_async_copy(dosage.at[pl.ds(at, rows), :], here, ready))
            copies[-1].start()
    for copy in copies:
        copy.wait()


def predict_body(quarters, scale, blocks, *refs):
    where = indices()
    pieces, (out, values) = refs[:quarters], refs[quarters:]
    place_values(quarters, where, pieces, values)
    chips, rows = out.shape[:2]
    for i in range(chips):
        block = blocks[i * rows : (i + 1) * rows, :]
        out[i] = jnp.dot(block, values[...], preferred_element_type=F32) * scale


def gradient_body(quarters, units, scale, *refs):
    where = indices()
    sides, pieces, outs = refs[:CORES], refs[CORES : -quarters - 2], refs[-quarters - 2 : -2]
    residual, total = refs[-2:]
    chips, rows = len(pieces) // CORES, pieces[0].shape[0]
    for i, piece in enumerate(pieces):
        residual[i * rows : (i + 1) * rows, :] = piece[...]
    turned = [residual[c * chips * rows : (c + 1) * chips * rows, :].T for c in range(CORES)]
    width = sides[0].shape[1] // units
    quarter_rows = width // quarters
    for u in range(units):
        product = jnp.dot(turned[0], sides[0][:, u * width : (u + 1) * width], preferred_element_type=F32)
        product += jnp.dot(turned[1], sides[1][:, u * width : (u + 1) * width], preferred_element_type=F32)
        total[u] = product.T * scale
        for k in range(quarters):
            at = pl.multiple_of((where[1] ^ k) * quarter_rows, quarter_rows)
            outs[k][u] = total[u, pl.ds(at, quarter_rows), :].astype(outs[k].dtype)


def leave_body(spot, quarters, pair, table, *refs):
    where = indices()
    sums, outs = refs[:quarters], refs[quarters:]
    for k in range(quarters):
        for p in range(pair):
            unit = table[spot.unit + held_by_seen(where[1] ^ k, where[0]) * pair + p]
            at = jnp.maximum(unit, 0)
            total = sums[0][at]
            for j in range(1, quarters):
                total = total + sums[j][at].astype(F32)
            outs[k][p] = jnp.where(unit >= 0, total, 0.0).astype(HALF)


def update_body(quarters, momenta, penalty, *refs):
    where = indices()
    last = len(momenta) == 1
    panels, pieces, states = refs[:quarters], refs[quarters : 2 * quarters], refs[2 * quarters : 3 * quarters]
    outs, gradient = refs[3 * quarters : -1], refs[-1]
    pair, quarter_rows = pieces[0].shape[:2]
    for k in range(quarters):
        for p in range(pair):
            at = p * quarters * quarter_rows + (where[1] ^ k) * quarter_rows
            gradient[pl.ds(pl.multiple_of(at, quarter_rows), quarter_rows), :] = pieces[k][p]
    for k in range(quarters):
        panel = panels[k][...].reshape(pair * quarter_rows, -1)
        direction = jnp.dot(panel, gradient[...], preferred_element_type=F32)
        direction = direction.reshape(pair, quarter_rows, -1)
        if last:
            point = states[k][...]
        else:
            now = states[k][0]
            point = now + momenta[0] * (now - states[k][1])
        stepped = point - direction
        size = jnp.maximum(jnp.abs(stepped) - penalty[...], 0.0)
        updated = jnp.where(stepped > 0, size, jnp.where(stepped < 0, -size, 0.0))
        if last:
            outs[k][...] = updated
        else:
            following = updated + momenta[1] * (updated - now)
            outs[k][...] = following
            outs[quarters + k][...] = following.astype(HALF)


def finish_body(spot, pair, table, *refs):
    where = indices()
    pieces, out, held = refs[:-2], refs[-2], refs[-1]
    for k, piece in enumerate(pieces):
        held[k] = piece[...]
    for slot in range(out.shape[0]):
        code = table[spot.code_of_slot + slot]
        known = jnp.maximum(code, 0)
        block = held[held_by(lax.div(known, pair), where[0]) ^ where[1], lax.rem(known, pair)]
        out[slot] = jnp.where(code >= 0, block, 0.0)


def steps(dosage, traits, coef_now, coef_prev, block_inverse, penalty, block_start, unit_owner):
    owners = lax.axis_size("var")
    quarters = lax.axis_size("samp")
    capacity, quarter_rows, right_cols = coef_now.shape
    block_most, unit_rows = block_inverse.shape[2:]
    per_device = dosage.shape[1] // unit_rows
    pair = min(block_most, per_device)
    reach = capacity // pair
    assert reach == quarters and owners % CORES == 0 and owners & (owners - 1) == 0
    chips = owners // CORES
    rows = dosage.shape[0] // owners
    codes = reach * pair
    inv_scale = 1.0 / math.sqrt(dosage.shape[1] * owners)
    grad_scale = 0.5 / math.sqrt(dosage.shape[0] * quarters)
    spot = Layout(codes, capacity, per_device)
    ranks = range(quarters)
    piece = (pair, quarter_rows, right_cols)
    share = (per_device, quarter_rows, right_cols)

    table, *sent = pl.pallas_call(
        functools.partial(begin_body, spot, owners, reach, pair, per_device, MOMENTA[0]),
        name="begin",
        in_specs=[SMEM] * 2 + [FAR] * 2,
        out_specs=[SMEM] + [VMEM] * reach,
        out_shape=[like((spot.size,), jnp.int32)] + [like(piece, HALF)] * reach,
        scratch_shapes=[pltpu.VMEM(coef_now.shape, F32)] * 2 + [pltpu.SemaphoreType.DMA((2,))],
        compiler_params=pltpu.CompilerParams(vmem_limit_bytes=60 * MIB),
    )(block_start, unit_owner, coef_now, coef_prev)
    arrived = [shifted(sent[g], "var", -g - 1) for g in range(reach)]
    prepared = local(
        functools.partial(prepare_body, spot, quarters, pair),
        [table], [coef_now, coef_prev, block_inverse],
        [like((2, *piece), F32)] * quarters + [like((pair, *block_inverse.shape[1:]), HALF)] * quarters,
        [pltpu.VMEM(coef_now.shape, F32)] * 2 + [pltpu.SemaphoreType.DMA((2 + codes,))], limit=LARGE_PREPARE, far=3,
    )
    states, chosen = prepared[:quarters], prepared[quarters:]
    chosen = [chosen[0]] + [crossed(chosen[k], "samp", k) for k in ranks[1:-1]] + [chosen[-1]]
    penalty = penalty.reshape(1, 1, right_cols)

    for step in range(len(MOMENTA)):
        own = local(
            functools.partial(local_values_body, spot, pair, step > 0),
            [table], arrived, like(share, HALF),
            [pltpu.VMEM((reach, *piece), HALF)],
        )
        pieces = [own] + [crossed(own, "samp", k) for k in ranks[1:]]
        if step == 0:
            block = like((chips * rows, dosage.shape[1]), HALF)
            dosage, chosen[-1] = lax.optimization_barrier((own, dosage, chosen[-1]))[1:]
            kept_rows, given_rows = local(
                load_body, [], [dosage], [block, block],
                [pltpu.SemaphoreType.DMA((owners,))], limit=LARGE, far=1,
            )
            chosen[-1] = crossed(chosen[-1], "samp", quarters - 1)
            pieces, kept_rows, given_rows, states = lax.optimization_barrier((pieces, kept_rows, given_rows, states))
            states = [states[0]] + [crossed(states[k], "samp", k) for k in ranks[1:]]
        buffers = [pltpu.VMEM((dosage.shape[1], right_cols), HALF)]
        half = like((chips, rows, right_cols), F32)
        flops = dosage.shape[0] * dosage.shape[1] * right_cols
        given, kept = (
            local(
                functools.partial(predict_body, quarters, inv_scale),
                [], [side, *pieces], half, buffers, limit=8, flops=flops,
            )
            for side in (given_rows, kept_rows)
        )
        given = crossed(given, "var", 1)
        both = kept + given
        total = both[0]
        for i in range(1, chips):
            total = total + crossed(both[i].astype(HALF), "var", CORES * i).astype(F32)
        residual_b = (total - traits).astype(HALF)
        mine = [residual_b] + [crossed(residual_b, "var", CORES * i) for i in range(1, chips)]
        others = [crossed(block, "var", 1) for block in mine]
        sums = local(
            functools.partial(gradient_body, quarters, per_device, grad_scale),
            [], [kept_rows, given_rows, *mine, *others],
            [like(share, F32 if k == 0 else HALF) for k in ranks],
            [
                pltpu.VMEM((dosage.shape[0], right_cols), HALF),
                pltpu.VMEM((per_device, unit_rows, right_cols), F32),
            ], limit=15, flops=2 * dosage.shape[0] * dosage.shape[1] * right_cols,
        )
        if step == len(MOMENTA) - 1:
            residual = lax.optimization_barrier((sums[0], total))[1] - traits
        sums = [sums[0]] + [crossed(sums[k], "samp", k) for k in ranks[1:]]
        leaving = local(
            functools.partial(leave_body, spot, quarters, pair),
            [table], sums, [like(piece, HALF)] * quarters,
        )
        landed = [to_owners(leaving[k], k) for k in ranks]
        if step == 0:
            chosen = lax.optimization_barrier((leaving, chosen))[1]
            panels = local(
                functools.partial(panels_body, spot, quarters, pair, block_most),
                [table],
                [part.reshape(pair, quarter_rows, block_most * unit_rows) for part in chosen],
                [like((pair, quarter_rows, block_most * unit_rows), HALF)] * quarters, limit=10,
            )
        last = step == len(MOMENTA) - 1
        outs = [like(piece, F32)] * quarters + ([] if last else [like(piece, HALF)] * quarters)
        result = local(
            functools.partial(update_body, quarters, MOMENTA[step : step + 2]),
            [], [penalty, *panels, *landed, *states], outs,
            [pltpu.VMEM((pair * unit_rows, right_cols), HALF)], limit=12,
            flops=2 * (pair * unit_rows) ** 2 * right_cols,
        )
        states = list(result[:quarters])
        if not last:
            arrived = [to_variants(result[quarters + k], k) for k in ranks]
    states = [states[0]] + [crossed(states[k], "samp", k) for k in ranks[1:]]
    current = local(
        functools.partial(finish_body, spot, pair),
        [table], states, like((capacity, quarter_rows, right_cols), F32),
        [pltpu.VMEM((quarters, *piece), F32)],
    )
    return (current, residual)


def solution(mesh):
    placed = (
        P("samp", "var"),
        P(("samp", "var"), None),
        P("var", "samp", None),
        P("var", "samp", None),
        P("var", "samp", None, None),
        P(),
        P(),
        P(),
    )
    return jax.shard_map(
        steps,
        mesh=mesh,
        in_specs=placed,
        out_specs=(P("var", "samp", None), P(("samp", "var"), None)),
        check_vma=False,
    )
```

```python
import functools
import math

import jax
import jax.numpy as jnp
from jax import lax
from jax.experimental import pallas as pl
from jax.experimental.pallas import tpu as pltpu
from jax.sharding import PartitionSpec as P


MOMENTA = (0.4, 0.55)
CORES = 2
MIB = 1 << 20
LARGE = 45
LARGE_CHOOSE = 57


SMEM = pl.BlockSpec(memory_space=pltpu.SMEM)
VMEM = pl.BlockSpec(memory_space=pltpu.VMEM)
FAR = pl.BlockSpec(memory_space=pl.ANY)
F32, HALF = jnp.float32, jnp.bfloat16


def like(shape, dtype):
    return jax.ShapeDtypeStruct(shape, dtype)


def local(body, scalars, arrays, outs, scratch=(), limit=8, flops=0, far=0):
    single = not isinstance(outs, list)
    moved = sum(math.prod(a.shape) * a.dtype.itemsize for a in [*arrays, *([outs] if single else outs)])
    return pl.pallas_call(
        body,
        in_specs=[SMEM] * len(scalars) + [FAR] * far + [VMEM] * (len(arrays) - far),
        out_specs=VMEM if single else [VMEM] * len(outs),
        out_shape=outs,
        scratch_shapes=list(scratch),
        compiler_params=pltpu.CompilerParams(vmem_limit_bytes=limit * MIB),
        cost_estimate=pl.CostEstimate(flops=flops, bytes_accessed=moved, transcendentals=0),
    )(*scalars, *arrays)


def indices():
    return [lax.axis_index(axis).astype(jnp.int32) for axis in ("var", "samp")]


def shifted(block, axis, distance):
    count = lax.axis_size(axis)
    return lax.ppermute(block, axis, [((i - distance) % count, i) for i in range(count)])


def crossed(block, axis, mask):
    count = lax.axis_size(axis)
    return lax.ppermute(block, axis, [(i, i ^ mask) for i in range(count)])


def held_by(group, owner):
    return group ^ (2 * (owner & 1))


def held_by_seen(rank, variant):
    return rank ^ (2 * ((variant + rank + 1) & 1))


def to_owners(block, mask):
    quarters, owners = lax.axis_size("samp"), lax.axis_size("var")
    route = [
        (s * owners + v, (s ^ mask) * owners + (v + held_by_seen(s ^ mask, v) + 1) % owners)
        for s in range(quarters)
        for v in range(owners)
    ]
    return lax.ppermute(block, ("samp", "var"), route)


def to_variants(block, mask):
    quarters, owners = lax.axis_size("samp"), lax.axis_size("var")
    route = [
        (s * owners + o, (s ^ mask) * owners + (o - held_by(s, o) - 1) % owners)
        for s in range(quarters)
        for o in range(owners)
    ]
    return lax.ppermute(block, ("samp", "var"), route)


class Layout:
    def __init__(self, codes, capacity, per_device):
        self.slot = 0
        self.live = self.slot + codes
        self.first = self.live + codes
        self.code_of_slot = self.first + codes
        self.local = self.code_of_slot + capacity
        self.unit = self.local + per_device
        self.size = self.unit + codes


def begin_body(spot, owners, reach, pair, per_device, momentum, start, owner, now, before, out, *refs):
    sent, (now_here, before_here, arrived) = refs[:reach], refs[reach:]
    copies = [
        pltpu.make_async_copy(now, now_here, arrived.at[0]),
        pltpu.make_async_copy(before, before_here, arrived.at[1]),
    ]
    for copy in copies:
        copy.start()
    tables_body(spot, owners, reach, pair, per_device, start, owner, out)
    for copy in copies:
        copy.wait()
    for g in range(reach):
        for p in range(pair):
            slot = out[spot.slot + g * pair + p]
            live = out[spot.live + g * pair + p]
            point = now_here[slot] + momentum * (now_here[slot] - before_here[slot])
            sent[g][p] = jnp.where(live == 1, point, 0.0).astype(HALF)


def tables_body(spot, owners, reach, pair, per_device, start, owner, out):
    where = indices()
    var = where[0]
    for i in range(spot.size):
        empty = spot.code_of_slot <= i < spot.local or i >= spot.unit
        out[i] = jnp.int32(-1 if empty else 0)
    devices = [lax.rem(var - gap + owners, owners) for gap in range(1, reach + 1)]
    owned = [
        [(owner[d * per_device + j] == var).astype(jnp.int32) for j in range(per_device)]
        for d in devices
    ]
    counts = [functools.reduce(lambda a, b: a + b, flags) for flags in owned]
    for g in range(reach):
        place = jnp.int32(0)
        first = jnp.int32(0)
        base = jnp.int32(0)
        for h in range(reach):
            if h != g:
                base = base + jnp.where(devices[h] < devices[g], counts[h], 0)
        for j in range(per_device):
            first = jnp.where(start[devices[g] * per_device + j] == 1, place, first)

            @pl.when(owned[g][j] == 1)
            def _():
                code = g * pair + place
                out[spot.slot + code] = base + place
                out[spot.live + code] = jnp.int32(1)
                out[spot.first + code] = first
                out[spot.code_of_slot + base + place] = code

            place = place + owned[g][j]
    mine = [owner[var * per_device + j] for j in range(per_device)]
    for j in range(per_device):
        gap = lax.rem(mine[j] - var + owners, owners)
        place = jnp.int32(0)
        for i in range(j):
            place = place + (mine[i] == mine[j]).astype(jnp.int32)
        code = (gap - 1) * pair + place
        out[spot.local + j] = code
        out[spot.unit + code] = jnp.int32(j)


def choose_body(spot, quarters, pair, table, inverses, *refs):
    where = indices()
    outs, arrived = refs[:quarters], refs[quarters]
    copies = []
    for k in range(quarters):
        for p in range(pair):
            slot = table[spot.slot + held_by(where[1] ^ k, where[0]) * pair + p]
            ready = arrived.at[k * pair + p]
            copies.append(pltpu.make_async_copy(inverses.at[slot], outs[k].at[p], ready))
            copies[-1].start()
    for copy in copies:
        copy.wait()


def states_body(spot, quarters, pair, table, now, before, *outs):
    where = indices()
    for k in range(quarters):
        for p in range(pair):
            code = held_by(where[1] ^ k, where[0]) * pair + p
            slot = table[spot.slot + code]
            live = table[spot.live + code] == 1
            outs[k][0, p] = jnp.where(live, now[slot], 0.0)
            outs[k][1, p] = jnp.where(live, before[slot], 0.0)


def panels_body(spot, quarters, pair, most, table, *refs):
    where = indices()
    panels, outs = refs[:quarters], refs[quarters:]
    width = panels[0].shape[2] // most
    row = held_by(where[1], where[0]) * pair
    for p in range(pair):
        first = table[spot.first + row + p]
        live = table[spot.live + row + p] == 1
        for q in range(pair):
            same = (table[spot.first + row + q] == first) & (table[spot.live + row + q] == 1)
            part = jnp.clip(q - first, 0, most - 1)
            columns = pl.ds(pl.multiple_of(part * width, width), width)
            for k in range(quarters):
                block = panels[k][p, :, columns]
                outs[k][p, :, q * width : (q + 1) * width] = jnp.where(same & live, block, jnp.zeros_like(block))


def local_values_body(spot, pair, turned, table, *refs):
    where = indices()
    pieces, out, held = refs[:-2], refs[-2], refs[-1]
    for k, piece in enumerate(pieces):
        held[k] = piece[...]
    for u in range(out.shape[0]):
        code = table[spot.local + u]
        group = lax.div(code, pair)
        at = (held_by_seen(group, where[0]) ^ where[1]) if turned else group
        out[u] = held[at, lax.rem(code, pair)]


def place_values(quarters, where, pieces, values):
    units, quarter_rows = pieces[0].shape[:2]
    for k in range(quarters):
        for u in range(units):
            at = u * quarters * quarter_rows + (where[1] ^ k) * quarter_rows
            values[pl.ds(pl.multiple_of(at, quarter_rows), quarter_rows), :] = pieces[k][u]


def load_body(dosage, *refs):
    where = indices()
    outs, arrived = refs[:CORES], refs[CORES]
    core, chip = lax.rem(where[0], CORES), lax.div(where[0], CORES)
    chips = arrived.shape[0] // CORES
    rows = outs[0].shape[0] // chips
    copies = []
    for c in reversed(range(CORES)):
        for i in range(chips):
            at = pl.multiple_of(((chip ^ i) * CORES + (core ^ c)) * rows, rows)
            here = outs[c].at[pl.ds(i * rows, rows), :]
            ready = arrived.at[c * chips + i]
            copies.append(pltpu.make_async_copy(dosage.at[pl.ds(at, rows), :], here, ready))
            copies[-1].start()
    for copy in copies:
        copy.wait()


def predict_body(quarters, scale, blocks, *refs):
    where = indices()
    pieces, (out, values) = refs[:quarters], refs[quarters:]
    place_values(quarters, where, pieces, values)
    chips, rows = out.shape[:2]
    for i in range(chips):
        block = blocks[i * rows : (i + 1) * rows, :]
        out[i] = jnp.dot(block, values[...], preferred_element_type=F32) * scale


def gradient_body(quarters, units, scale, *refs):
    where = indices()
    sides, pieces, outs = refs[:CORES], refs[CORES : -quarters - 2], refs[-quarters - 2 : -2]
    residual, total = refs[-2:]
    chips, rows = len(pieces) // CORES, pieces[0].shape[0]
    for i, piece in enumerate(pieces):
        residual[i * rows : (i + 1) * rows, :] = piece[...]
    turned = [residual[c * chips * rows : (c + 1) * chips * rows, :].T for c in range(CORES)]
    width = sides[0].shape[1] // units
    quarter_rows = width // quarters
    for u in range(units):
        product = jnp.dot(turned[0], sides[0][:, u * width : (u + 1) * width], preferred_element_type=F32)
        product += jnp.dot(turned[1], sides[1][:, u * width : (u + 1) * width], preferred_element_type=F32)
        total[u] = product.T * scale
        for k in range(quarters):
            at = pl.multiple_of((where[1] ^ k) * quarter_rows, quarter_rows)
            outs[k][u] = total[u, pl.ds(at, quarter_rows), :].astype(outs[k].dtype)


def leave_body(spot, quarters, pair, table, *refs):
    where = indices()
    sums, outs = refs[:quarters], refs[quarters:]
    for k in range(quarters):
        for p in range(pair):
            unit = table[spot.unit + held_by_seen(where[1] ^ k, where[0]) * pair + p]
            at = jnp.maximum(unit, 0)
            total = sums[0][at]
            for j in range(1, quarters):
                total = total + sums[j][at].astype(F32)
            outs[k][p] = jnp.where(unit >= 0, total, 0.0).astype(HALF)


def update_body(quarters, momenta, penalty, *refs):
    where = indices()
    last = len(momenta) == 1
    panels, pieces, states = refs[:quarters], refs[quarters : 2 * quarters], refs[2 * quarters : 3 * quarters]
    outs, gradient = refs[3 * quarters : -1], refs[-1]
    pair, quarter_rows = pieces[0].shape[:2]
    for k in range(quarters):
        for p in range(pair):
            at = p * quarters * quarter_rows + (where[1] ^ k) * quarter_rows
            gradient[pl.ds(pl.multiple_of(at, quarter_rows), quarter_rows), :] = pieces[k][p]
    for k in range(quarters):
        panel = panels[k][...].reshape(pair * quarter_rows, -1)
        direction = jnp.dot(panel, gradient[...], preferred_element_type=F32)
        direction = direction.reshape(pair, quarter_rows, -1)
        if last:
            point = states[k][...]
        else:
            now = states[k][0]
            point = now + momenta[0] * (now - states[k][1])
        stepped = point - direction
        size = jnp.maximum(jnp.abs(stepped) - penalty[...], 0.0)
        updated = jnp.where(stepped > 0, size, jnp.where(stepped < 0, -size, 0.0))
        if last:
            outs[k][...] = updated
        else:
            following = updated + momenta[1] * (updated - now)
            outs[k][...] = following
            outs[quarters + k][...] = following.astype(HALF)


def finish_body(spot, pair, table, *refs):
    where = indices()
    pieces, out, held = refs[:-2], refs[-2], refs[-1]
    for k, piece in enumerate(pieces):
        held[k] = piece[...]
    for slot in range(out.shape[0]):
        code = table[spot.code_of_slot + slot]
        known = jnp.maximum(code, 0)
        block = held[held_by(lax.div(known, pair), where[0]) ^ where[1], lax.rem(known, pair)]
        out[slot] = jnp.where(code >= 0, block, 0.0)


def steps(dosage, traits, coef_now, coef_prev, block_inverse, penalty, block_start, unit_owner):
    owners = lax.axis_size("var")
    quarters = lax.axis_size("samp")
    capacity, quarter_rows, right_cols = coef_now.shape
    block_most, unit_rows = block_inverse.shape[2:]
    per_device = dosage.shape[1] // unit_rows
    pair = min(block_most, per_device)
    reach = capacity // pair
    assert reach == quarters and owners % CORES == 0 and owners & (owners - 1) == 0
    chips = owners // CORES
    rows = dosage.shape[0] // owners
    codes = reach * pair
    inv_scale = 1.0 / math.sqrt(dosage.shape[1] * owners)
    grad_scale = 0.5 / math.sqrt(dosage.shape[0] * quarters)
    spot = Layout(codes, capacity, per_device)
    ranks = range(quarters)
    piece = (pair, quarter_rows, right_cols)
    share = (per_device, quarter_rows, right_cols)

    table, *sent = pl.pallas_call(
        functools.partial(begin_body, spot, owners, reach, pair, per_device, MOMENTA[0]),
        name="begin",
        in_specs=[SMEM] * 2 + [FAR] * 2,
        out_specs=[SMEM] + [VMEM] * reach,
        out_shape=[like((spot.size,), jnp.int32)] + [like(piece, HALF)] * reach,
        scratch_shapes=[pltpu.VMEM(coef_now.shape, F32)] * 2 + [pltpu.SemaphoreType.DMA((2,))],
        compiler_params=pltpu.CompilerParams(vmem_limit_bytes=60 * MIB),
    )(block_start, unit_owner, coef_now, coef_prev)
    arrived = [shifted(sent[g], "var", -g - 1) for g in range(reach)]
    chosen = local(
        functools.partial(choose_body, spot, quarters, pair),
        [table], [block_inverse], [like((pair, *block_inverse.shape[1:]), HALF)] * quarters,
        [pltpu.SemaphoreType.DMA((codes,))], limit=LARGE_CHOOSE, far=1,
    )
    block = like((chips * rows, dosage.shape[1]), HALF)
    dosage = lax.optimization_barrier((chosen[0], dosage))[1]
    kept_rows, given_rows = local(
        load_body, [], [dosage], [block, block], [pltpu.SemaphoreType.DMA((owners,))], limit=LARGE, far=1
    )
    arrived, chosen, kept_rows, given_rows = lax.optimization_barrier(
        (arrived, chosen, kept_rows, given_rows)
    )
    chosen = [chosen[0]] + [crossed(chosen[k], "samp", k) for k in ranks[1:]]
    penalty = penalty.reshape(1, 1, right_cols)

    for step in range(len(MOMENTA)):
        own = local(
            functools.partial(local_values_body, spot, pair, step > 0),
            [table], arrived, like(share, HALF),
            [pltpu.VMEM((reach, *piece), HALF)],
        )
        pieces = [own] + [crossed(own, "samp", k) for k in ranks[1:]]
        buffers = [pltpu.VMEM((dosage.shape[1], right_cols), HALF)]
        half = like((chips, rows, right_cols), F32)
        flops = dosage.shape[0] * dosage.shape[1] * right_cols
        given, kept = (
            local(
                functools.partial(predict_body, quarters, inv_scale),
                [], [side, *pieces], half, buffers, limit=8, flops=flops,
            )
            for side in (given_rows, kept_rows)
        )
        given = crossed(given, "var", 1)
        both = kept + given
        total = both[0]
        for i in range(1, chips):
            total = total + crossed(both[i].astype(HALF), "var", CORES * i).astype(F32)
        residual_b = (total - traits).astype(HALF)
        mine = [residual_b] + [crossed(residual_b, "var", CORES * i) for i in range(1, chips)]
        others = [crossed(block, "var", 1) for block in mine]
        sums = local(
            functools.partial(gradient_body, quarters, per_device, grad_scale),
            [], [kept_rows, given_rows, *mine, *others],
            [like(share, F32 if k == 0 else HALF) for k in ranks],
            [
                pltpu.VMEM((dosage.shape[0], right_cols), HALF),
                pltpu.VMEM((per_device, unit_rows, right_cols), F32),
            ], limit=15, flops=2 * dosage.shape[0] * dosage.shape[1] * right_cols,
        )
        if step == len(MOMENTA) - 1:
            residual = lax.optimization_barrier((sums[0], total))[1] - traits
        summed = sums[0]
        sums = [summed] + [crossed(sums[k], "samp", k) for k in ranks[1:]]
        if step == 0:
            held = lax.optimization_barrier((summed, coef_now, coef_prev))[1:]
            states = local(
                functools.partial(states_body, spot, quarters, pair),
                [table], list(held), [like((2, *piece), F32)] * quarters,
            )
            states = [states[0]] + [crossed(states[k], "samp", k) for k in ranks[1:]]
        leaving = local(
            functools.partial(leave_body, spot, quarters, pair),
            [table], sums, [like(piece, HALF)] * quarters,
        )
        landed = [to_owners(leaving[k], k) for k in ranks]
        if step == 0:
            chosen = lax.optimization_barrier((leaving, chosen))[1]
            panels = local(
                functools.partial(panels_body, spot, quarters, pair, block_most),
                [table],
                [part.reshape(pair, quarter_rows, block_most * unit_rows) for part in chosen],
                [like((pair, quarter_rows, block_most * unit_rows), HALF)] * quarters, limit=10,
            )
        last = step == len(MOMENTA) - 1
        outs = [like(piece, F32)] * quarters + ([] if last else [like(piece, HALF)] * quarters)
        result = local(
            functools.partial(update_body, quarters, MOMENTA[step : step + 2]),
            [], [penalty, *panels, *landed, *states], outs,
            [pltpu.VMEM((pair * unit_rows, right_cols), HALF)], limit=12,
            flops=2 * (pair * unit_rows) ** 2 * right_cols,
        )
        states = list(result[:quarters])
        if not last:
            arrived = [to_variants(result[quarters + k], k) for k in ranks]
    states = [states[0]] + [crossed(states[k], "samp", k) for k in ranks[1:]]
    current = local(
        functools.partial(finish_body, spot, pair),
        [table], states, like((capacity, quarter_rows, right_cols), F32),
        [pltpu.VMEM((quarters, *piece), F32)],
    )
    return (current, residual)


def solution(mesh):
    placed = (
        P("samp", "var"),
        P(("samp", "var"), None),
        P("var", "samp", None),
        P("var", "samp", None),
        P("var", "samp", None, None),
        P(),
        P(),
        P(),
    )
    return jax.shard_map(
        steps,
        mesh=mesh,
        in_specs=placed,
        out_specs=(P("var", "samp", None), P(("samp", "var"), None)),
        check_vma=False,
    )
```

```python
import functools
import math

import jax
import jax.numpy as jnp
from jax import lax
from jax.experimental import pallas as pl
from jax.experimental.pallas import tpu as pltpu
from jax.sharding import PartitionSpec as P


MOMENTA = (0.4, 0.55)
CORES = 2
MIB = 1 << 20
LARGE = 45
LARGE_FIRST = 46
LARGE_CHOOSE = 57


SMEM = pl.BlockSpec(memory_space=pltpu.SMEM)
VMEM = pl.BlockSpec(memory_space=pltpu.VMEM)
FAR = pl.BlockSpec(memory_space=pl.ANY)
F32, HALF = jnp.float32, jnp.bfloat16


def like(shape, dtype):
    return jax.ShapeDtypeStruct(shape, dtype)


def local(body, scalars, arrays, outs, scratch=(), limit=8, flops=0, far=0):
    single = not isinstance(outs, list)
    moved = sum(math.prod(a.shape) * a.dtype.itemsize for a in [*arrays, *([outs] if single else outs)])
    return pl.pallas_call(
        body,
        in_specs=[SMEM] * len(scalars) + [FAR] * far + [VMEM] * (len(arrays) - far),
        out_specs=VMEM if single else [VMEM] * len(outs),
        out_shape=outs,
        scratch_shapes=list(scratch),
        compiler_params=pltpu.CompilerParams(vmem_limit_bytes=limit * MIB),
        cost_estimate=pl.CostEstimate(flops=flops, bytes_accessed=moved, transcendentals=0),
    )(*scalars, *arrays)


def indices():
    return [lax.axis_index(axis).astype(jnp.int32) for axis in ("var", "samp")]


def shifted(block, axis, distance):
    count = lax.axis_size(axis)
    return lax.ppermute(block, axis, [((i - distance) % count, i) for i in range(count)])


def crossed(block, axis, mask):
    count = lax.axis_size(axis)
    return lax.ppermute(block, axis, [(i, i ^ mask) for i in range(count)])


def held_by(group, owner):
    return group ^ (2 * (owner & 1))


def held_by_seen(rank, variant):
    return rank ^ (2 * ((variant + rank + 1) & 1))


def fan(send, blocks, ranks):
    sent = []
    for k in ranks:
        sent.append(send(blocks[k], k))
    return sent


def over_samp(block, mask):
    return crossed(block, "samp", mask)


def over_chips(block, mask):
    return crossed(block, "var", CORES * mask)


def to_owners(block, mask):
    quarters, owners = lax.axis_size("samp"), lax.axis_size("var")
    route = [
        (s * owners + v, (s ^ mask) * owners + (v + held_by_seen(s ^ mask, v) + 1) % owners)
        for s in range(quarters)
        for v in range(owners)
    ]
    return lax.ppermute(block, ("samp", "var"), route)


def to_variants(block, mask):
    quarters, owners = lax.axis_size("samp"), lax.axis_size("var")
    route = [
        (s * owners + o, (s ^ mask) * owners + (o - held_by(s, o) - 1) % owners)
        for s in range(quarters)
        for o in range(owners)
    ]
    return lax.ppermute(block, ("samp", "var"), route)


class Layout:
    def __init__(self, codes, capacity, per_device):
        self.slot = 0
        self.live = self.slot + codes
        self.first = self.live + codes
        self.code_of_slot = self.first + codes
        self.local = self.code_of_slot + capacity
        self.unit = self.local + per_device
        self.size = self.unit + codes


def begin_body(spot, owners, reach, pair, per_device, momentum, start, owner, now, before, out, *refs):
    sent, (now_here, before_here, arrived) = refs[:reach], refs[reach:]
    copies = [
        pltpu.make_async_copy(now, now_here, arrived.at[0]),
        pltpu.make_async_copy(before, before_here, arrived.at[1]),
    ]
    for copy in copies:
        copy.start()
    tables_body(spot, owners, reach, pair, per_device, start, owner, out)
    for copy in copies:
        copy.wait()
    for g in range(reach):
        for p in range(pair):
            slot = out[spot.slot + g * pair + p]
            live = out[spot.live + g * pair + p]
            point = now_here[slot] + momentum * (now_here[slot] - before_here[slot])
            sent[g][p] = jnp.where(live == 1, point, 0.0).astype(HALF)


def tables_body(spot, owners, reach, pair, per_device, start, owner, out):
    where = indices()
    var = where[0]
    for i in range(spot.size):
        empty = spot.code_of_slot <= i < spot.local or i >= spot.unit
        out[i] = jnp.int32(-1 if empty else 0)
    devices = [lax.rem(var - gap + owners, owners) for gap in range(1, reach + 1)]
    owned = [
        [(owner[d * per_device + j] == var).astype(jnp.int32) for j in range(per_device)]
        for d in devices
    ]
    counts = [functools.reduce(lambda a, b: a + b, flags) for flags in owned]
    for g in range(reach):
        place = jnp.int32(0)
        first = jnp.int32(0)
        base = jnp.int32(0)
        for h in range(reach):
            if h != g:
                base = base + jnp.where(devices[h] < devices[g], counts[h], 0)
        for j in range(per_device):
            first = jnp.where(start[devices[g] * per_device + j] == 1, place, first)

            @pl.when(owned[g][j] == 1)
            def _():
                code = g * pair + place
                out[spot.slot + code] = base + place
                out[spot.live + code] = jnp.int32(1)
                out[spot.first + code] = first
                out[spot.code_of_slot + base + place] = code

            place = place + owned[g][j]
    mine = [owner[var * per_device + j] for j in range(per_device)]
    for j in range(per_device):
        gap = lax.rem(mine[j] - var + owners, owners)
        place = jnp.int32(0)
        for i in range(j):
            place = place + (mine[i] == mine[j]).astype(jnp.int32)
        code = (gap - 1) * pair + place
        out[spot.local + j] = code
        out[spot.unit + code] = jnp.int32(j)


def choose_body(spot, quarters, pair, table, inverses, *refs):
    where = indices()
    outs, arrived = refs[:quarters], refs[quarters]
    copies = []
    for k in range(quarters):
        for p in range(pair):
            slot = table[spot.slot + held_by(where[1] ^ k, where[0]) * pair + p]
            ready = arrived.at[k * pair + p]
            copies.append(pltpu.make_async_copy(inverses.at[slot], outs[k].at[p], ready))
            copies[-1].start()
    for copy in copies:
        copy.wait()


def states_body(spot, quarters, pair, momentum, table, now, before, *outs):
    where = indices()
    for k in range(quarters):
        for p in range(pair):
            code = held_by(where[1] ^ k, where[0]) * pair + p
            slot = table[spot.slot + code]
            live = table[spot.live + code] == 1
            held = jnp.where(live, now[slot], 0.0)
            point = held + momentum * (held - jnp.where(live, before[slot], 0.0))
            high = point.astype(HALF)
            outs[k][0, p] = high
            outs[k][1, p] = (point - high.astype(F32)).astype(HALF)
            outs[k][2, p] = held.astype(HALF)


def panels_body(spot, quarters, pair, most, table, *refs):
    where = indices()
    panels, outs = refs[:quarters], refs[quarters:]
    width = panels[0].shape[2] // most
    row = held_by(where[1], where[0]) * pair
    for p in range(pair):
        first = table[spot.first + row + p]
        live = table[spot.live + row + p] == 1
        for q in range(pair):
            same = (table[spot.first + row + q] == first) & (table[spot.live + row + q] == 1)
            part = jnp.clip(q - first, 0, most - 1)
            columns = pl.ds(pl.multiple_of(part * width, width), width)
            for k in range(quarters):
                block = panels[k][p, :, columns]
                outs[k][p, :, q * width : (q + 1) * width] = jnp.where(same & live, block, jnp.zeros_like(block))


def local_values_body(spot, pair, turned, table, *refs):
    where = indices()
    pieces, out, held = refs[:-2], refs[-2], refs[-1]
    for k, piece in enumerate(pieces):
        held[k] = piece[...]
    for u in range(out.shape[0]):
        code = table[spot.local + u]
        group = lax.div(code, pair)
        at = (held_by_seen(group, where[0]) ^ where[1]) if turned else group
        out[u] = held[at, lax.rem(code, pair)]


def place_values(quarters, where, pieces, values):
    units, quarter_rows = pieces[0].shape[:2]
    for k in range(quarters):
        for u in range(units):
            at = u * quarters * quarter_rows + (where[1] ^ k) * quarter_rows
            values[pl.ds(pl.multiple_of(at, quarter_rows), quarter_rows), :] = pieces[k][u]


def load_body(partner, dosage, out, arrived):
    where = indices()
    core, chip = lax.rem(where[0], CORES), lax.div(where[0], CORES)
    chips = arrived.shape[0]
    rows = out.shape[0] // chips
    copies = []
    for i in range(chips):
        at = pl.multiple_of(((chip ^ i) * CORES + (core ^ partner)) * rows, rows)
        copies.append(
            pltpu.make_async_copy(dosage.at[pl.ds(at, rows), :], out.at[pl.ds(i * rows, rows), :], arrived.at[i])
        )
        copies[-1].start()
    for copy in copies:
        copy.wait()


def predict_body(quarters, scale, blocks, *refs):
    where = indices()
    pieces, (out, values) = refs[:quarters], refs[quarters:]
    place_values(quarters, where, pieces, values)
    chips, rows = out.shape[:2]
    for i in range(chips):
        block = blocks[i * rows : (i + 1) * rows, :]
        out[i] = jnp.dot(block, values[...], preferred_element_type=F32) * scale


def gradient_body(quarters, units, scale, *refs):
    where = indices()
    sides, pieces, outs = refs[:CORES], refs[CORES : -quarters - 2], refs[-quarters - 2 : -2]
    residual, total = refs[-2:]
    chips, rows = len(pieces) // CORES, pieces[0].shape[0]
    for i, piece in enumerate(pieces):
        residual[i * rows : (i + 1) * rows, :] = piece[...]
    turned = [residual[c * chips * rows : (c + 1) * chips * rows, :].T for c in range(CORES)]
    width = sides[0].shape[1] // units
    quarter_rows = width // quarters
    for u in range(units):
        product = jnp.dot(turned[0], sides[0][:, u * width : (u + 1) * width], preferred_element_type=F32)
        product += jnp.dot(turned[1], sides[1][:, u * width : (u + 1) * width], preferred_element_type=F32)
        total[u] = product.T * scale
        for k in range(quarters):
            at = pl.multiple_of((where[1] ^ k) * quarter_rows, quarter_rows)
            outs[k][u] = total[u, pl.ds(at, quarter_rows), :].astype(outs[k].dtype)


def leave_body(spot, quarters, pair, table, *refs):
    where = indices()
    sums, outs = refs[:quarters], refs[quarters:]
    for k in range(quarters):
        for p in range(pair):
            unit = table[spot.unit + held_by_seen(where[1] ^ k, where[0]) * pair + p]
            at = jnp.maximum(unit, 0)
            total = sums[0][at]
            for j in range(1, quarters):
                total = total + sums[j][at].astype(F32)
            outs[k][p] = jnp.where(unit >= 0, total, 0.0).astype(HALF)


def update_body(quarters, momentum, penalty, *refs):
    where = indices()
    last = momentum is None
    panels, pieces, states = refs[:quarters], refs[quarters : 2 * quarters], refs[2 * quarters : 3 * quarters]
    outs, gradient = refs[3 * quarters : -1], refs[-1]
    pair, quarter_rows = pieces[0].shape[:2]
    for k in range(quarters):
        for p in range(pair):
            at = p * quarters * quarter_rows + (where[1] ^ k) * quarter_rows
            gradient[pl.ds(pl.multiple_of(at, quarter_rows), quarter_rows), :] = pieces[k][p]
    for k in range(quarters):
        panel = panels[k][...].reshape(pair * quarter_rows, -1)
        direction = jnp.dot(panel, gradient[...], preferred_element_type=F32)
        direction = direction.reshape(pair, quarter_rows, -1)
        if last:
            point = states[k][...]
        else:
            point = states[k][0].astype(F32) + states[k][1].astype(F32)
            now = states[k][2].astype(F32)
        stepped = point - direction
        size = jnp.maximum(jnp.abs(stepped) - penalty[...], 0.0)
        updated = jnp.where(stepped > 0, size, jnp.where(stepped < 0, -size, 0.0))
        if last:
            outs[k][...] = updated
        else:
            following = updated + momentum * (updated - now)
            outs[k][...] = following
            outs[quarters + k][...] = following.astype(HALF)


def finish_body(spot, pair, table, *refs):
    where = indices()
    pieces, out, held = refs[:-2], refs[-2], refs[-1]
    for k, piece in enumerate(pieces):
        held[k] = piece[...]
    for slot in range(out.shape[0]):
        code = table[spot.code_of_slot + slot]
        known = jnp.maximum(code, 0)
        block = held[held_by(lax.div(known, pair), where[0]) ^ where[1], lax.rem(known, pair)]
        out[slot] = jnp.where(code >= 0, block, 0.0)


def steps(dosage, traits, coef_now, coef_prev, block_inverse, penalty, block_start, unit_owner):
    owners = lax.axis_size("var")
    quarters = lax.axis_size("samp")
    capacity, quarter_rows, right_cols = coef_now.shape
    block_most, unit_rows = block_inverse.shape[2:]
    per_device = dosage.shape[1] // unit_rows
    pair = min(block_most, per_device)
    reach = capacity // pair
    assert reach == quarters and owners % CORES == 0 and owners & (owners - 1) == 0
    chips = owners // CORES
    rows = dosage.shape[0] // owners
    codes = reach * pair
    inv_scale = 1.0 / math.sqrt(dosage.shape[1] * owners)
    grad_scale = 0.5 / math.sqrt(dosage.shape[0] * quarters)
    spot = Layout(codes, capacity, per_device)
    ranks = range(quarters)
    piece = (pair, quarter_rows, right_cols)
    share = (per_device, quarter_rows, right_cols)

    table, *sent = pl.pallas_call(
        functools.partial(begin_body, spot, owners, reach, pair, per_device, MOMENTA[0]),
        name="begin",
        in_specs=[SMEM] * 2 + [FAR] * 2,
        out_specs=[SMEM] + [VMEM] * reach,
        out_shape=[like((spot.size,), jnp.int32)] + [like(piece, HALF)] * reach,
        scratch_shapes=[pltpu.VMEM(coef_now.shape, F32)] * 2 + [pltpu.SemaphoreType.DMA((2,))],
        compiler_params=pltpu.CompilerParams(vmem_limit_bytes=60 * MIB),
    )(block_start, unit_owner, coef_now, coef_prev)
    arrived = [shifted(sent[g], "var", -g - 1) for g in range(reach)]
    chosen = local(
        functools.partial(choose_body, spot, quarters, pair),
        [table], [block_inverse], [like((pair, *block_inverse.shape[1:]), HALF)] * quarters,
        [pltpu.SemaphoreType.DMA((codes,))], limit=LARGE_CHOOSE, far=1,
    )
    block = like((chips * rows, dosage.shape[1]), HALF)
    later = lax.optimization_barrier((chosen[0], dosage))[1]
    given_rows = local(
        functools.partial(load_body, 1), [], [later], block,
        [pltpu.SemaphoreType.DMA((chips,))], limit=LARGE_FIRST, far=1,
    )
    arrived, chosen, given_rows = lax.optimization_barrier((arrived, chosen, given_rows))
    chosen = [chosen[0]] + [crossed(chosen[k], "samp", k) for k in ranks[1:]]
    penalty = penalty.reshape(1, 1, right_cols)

    for step in range(len(MOMENTA)):
        own = local(
            functools.partial(local_values_body, spot, pair, step > 0),
            [table], arrived, like(share, HALF),
            [pltpu.VMEM((reach, *piece), HALF)],
        )
        pieces = [own] + [crossed(own, "samp", k) for k in ranks[1:]]
        if step == 0:
            later = lax.optimization_barrier((own, dosage))[1]
            kept_rows = local(
                functools.partial(load_body, 0), [], [later], block,
                [pltpu.SemaphoreType.DMA((chips,))], limit=LARGE, far=1,
            )
            pieces, kept_rows = lax.optimization_barrier((pieces, kept_rows))
        buffers = [pltpu.VMEM((dosage.shape[1], right_cols), HALF)]
        half = like((chips, rows, right_cols), F32)
        flops = dosage.shape[0] * dosage.shape[1] * right_cols
        given, kept = (
            local(
                functools.partial(predict_body, quarters, inv_scale),
                [], [side, *pieces], half, buffers, limit=8, flops=flops,
            )
            for side in (given_rows, kept_rows)
        )
        given = crossed(given, "var", 1)
        both = kept + given
        total = both[0]
        for part in fan(over_chips, both.astype(HALF), range(1, chips)):
            total = total + part.astype(F32)
        residual_b = (total - traits).astype(HALF)
        mine = [residual_b] + fan(over_chips, [residual_b] * chips, range(1, chips))
        others = [crossed(block, "var", 1) for block in mine]
        sums = local(
            functools.partial(gradient_body, quarters, per_device, grad_scale),
            [], [kept_rows, given_rows, *mine, *others],
            [like(share, F32 if k == 0 else HALF) for k in ranks],
            [
                pltpu.VMEM((dosage.shape[0], right_cols), HALF),
                pltpu.VMEM((per_device, unit_rows, right_cols), F32),
            ], limit=15, flops=2 * dosage.shape[0] * dosage.shape[1] * right_cols,
        )
        if step == len(MOMENTA) - 1:
            residual = lax.optimization_barrier((sums[0], total))[1] - traits
        summed = sums[0]
        sums = [summed] + fan(over_samp, sums, ranks[1:])
        if step == 0:
            held = lax.optimization_barrier((summed, coef_now, coef_prev))[1:]
            states = local(
                functools.partial(states_body, spot, quarters, pair, MOMENTA[0]),
                [table], list(held), [like((3, *piece), HALF)] * quarters,
            )
            states = [states[0]] + [crossed(states[k], "samp", k) for k in ranks[1:]]
        leaving = local(
            functools.partial(leave_body, spot, quarters, pair),
            [table], sums, [like(piece, HALF)] * quarters,
        )
        landed = [to_owners(leaving[k], k) for k in ranks]
        if step == 0:
            chosen = lax.optimization_barrier((leaving, chosen))[1]
            panels = local(
                functools.partial(panels_body, spot, quarters, pair, block_most),
                [table],
                [part.reshape(pair, quarter_rows, block_most * unit_rows) for part in chosen],
                [like((pair, quarter_rows, block_most * unit_rows), HALF)] * quarters, limit=10,
            )
        last = step == len(MOMENTA) - 1
        outs = [like(piece, F32)] * quarters + ([] if last else [like(piece, HALF)] * quarters)
        result = local(
            functools.partial(update_body, quarters, None if last else MOMENTA[step + 1]),
            [], [penalty, *panels, *landed, *states], outs,
            [pltpu.VMEM((pair * unit_rows, right_cols), HALF)], limit=12,
            flops=2 * (pair * unit_rows) ** 2 * right_cols,
        )
        states = list(result[:quarters])
        if not last:
            arrived = fan(to_variants, result[quarters:], ranks)
    states = [states[0]] + fan(over_samp, states, ranks[1:])
    current = local(
        functools.partial(finish_body, spot, pair),
        [table], states, like((capacity, quarter_rows, right_cols), F32),
        [pltpu.VMEM((quarters, *piece), F32)],
    )
    return (current, residual)


def solution(mesh):
    placed = (
        P("samp", "var"),
        P(("samp", "var"), None),
        P("var", "samp", None),
        P("var", "samp", None),
        P("var", "samp", None, None),
        P(),
        P(),
        P(),
    )
    return jax.shard_map(
        steps,
        mesh=mesh,
        in_specs=placed,
        out_specs=(P("var", "samp", None), P(("samp", "var"), None)),
        check_vma=False,
    )
```

```python
import functools
import math

import jax
import jax.numpy as jnp
from jax import lax
from jax.experimental import pallas as pl
from jax.experimental.pallas import tpu as pltpu
from jax.sharding import PartitionSpec as P


MOMENTA = (0.4, 0.55)
CORES = 2
MIB = 1 << 20
LARGE = 45
LARGE_FIRST = 46
LARGE_CHOOSE = 57


SMEM = pl.BlockSpec(memory_space=pltpu.SMEM)
VMEM = pl.BlockSpec(memory_space=pltpu.VMEM)
FAR = pl.BlockSpec(memory_space=pl.ANY)
F32, HALF = jnp.float32, jnp.bfloat16


def like(shape, dtype):
    return jax.ShapeDtypeStruct(shape, dtype)


def local(body, scalars, arrays, outs, scratch=(), limit=8, flops=0, far=0):
    single = not isinstance(outs, list)
    moved = sum(math.prod(a.shape) * a.dtype.itemsize for a in [*arrays, *([outs] if single else outs)])
    return pl.pallas_call(
        body,
        in_specs=[SMEM] * len(scalars) + [FAR] * far + [VMEM] * (len(arrays) - far),
        out_specs=VMEM if single else [VMEM] * len(outs),
        out_shape=outs,
        scratch_shapes=list(scratch),
        compiler_params=pltpu.CompilerParams(vmem_limit_bytes=limit * MIB),
        cost_estimate=pl.CostEstimate(flops=flops, bytes_accessed=moved, transcendentals=0),
    )(*scalars, *arrays)


def indices():
    return [lax.axis_index(axis).astype(jnp.int32) for axis in ("var", "samp")]


def shifted(block, axis, distance):
    count = lax.axis_size(axis)
    return lax.ppermute(block, axis, [((i - distance) % count, i) for i in range(count)])


def crossed(block, axis, mask):
    count = lax.axis_size(axis)
    return lax.ppermute(block, axis, [(i, i ^ mask) for i in range(count)])


def held_by(group, owner):
    return group ^ (2 * (owner & 1))


def held_by_seen(rank, variant):
    return rank ^ (2 * ((variant + rank + 1) & 1))


def fan(send, blocks, ranks):
    sent = []
    for k in ranks:
        sent.append(send(blocks[k], k))
    return sent


def over_samp(block, mask):
    return crossed(block, "samp", mask)


def over_chips(block, mask):
    return crossed(block, "var", CORES * mask)


def to_owners(block, mask):
    quarters, owners = lax.axis_size("samp"), lax.axis_size("var")
    route = [
        (s * owners + v, (s ^ mask) * owners + (v + held_by_seen(s ^ mask, v) + 1) % owners)
        for s in range(quarters)
        for v in range(owners)
    ]
    return lax.ppermute(block, ("samp", "var"), route)


def to_variants(block, mask):
    quarters, owners = lax.axis_size("samp"), lax.axis_size("var")
    route = [
        (s * owners + o, (s ^ mask) * owners + (o - held_by(s, o) - 1) % owners)
        for s in range(quarters)
        for o in range(owners)
    ]
    return lax.ppermute(block, ("samp", "var"), route)


class Layout:
    def __init__(self, codes, capacity, per_device):
        self.slot = 0
        self.live = self.slot + codes
        self.first = self.live + codes
        self.code_of_slot = self.first + codes
        self.local = self.code_of_slot + capacity
        self.unit = self.local + per_device
        self.size = self.unit + codes


def begin_body(spot, owners, reach, pair, per_device, momentum, start, owner, now, before, out, *refs):
    sent, (now_here, before_here, arrived) = refs[:reach], refs[reach:]
    copies = [
        pltpu.make_async_copy(now, now_here, arrived.at[0]),
        pltpu.make_async_copy(before, before_here, arrived.at[1]),
    ]
    for copy in copies:
        copy.start()
    tables_body(spot, owners, reach, pair, per_device, start, owner, out)
    for copy in copies:
        copy.wait()
    for g in range(reach):
        for p in range(pair):
            slot = out[spot.slot + g * pair + p]
            live = out[spot.live + g * pair + p]
            point = now_here[slot] + momentum * (now_here[slot] - before_here[slot])
            sent[g][p] = jnp.where(live == 1, point, 0.0).astype(HALF)


def tables_body(spot, owners, reach, pair, per_device, start, owner, out):
    where = indices()
    var = where[0]
    for i in range(spot.size):
        empty = spot.code_of_slot <= i < spot.local or i >= spot.unit
        out[i] = jnp.int32(-1 if empty else 0)
    devices = [lax.rem(var - gap + owners, owners) for gap in range(1, reach + 1)]
    owned = [
        [(owner[d * per_device + j] == var).astype(jnp.int32) for j in range(per_device)]
        for d in devices
    ]
    counts = [functools.reduce(lambda a, b: a + b, flags) for flags in owned]
    for g in range(reach):
        place = jnp.int32(0)
        first = jnp.int32(0)
        base = jnp.int32(0)
        for h in range(reach):
            if h != g:
                base = base + jnp.where(devices[h] < devices[g], counts[h], 0)
        for j in range(per_device):
            first = jnp.where(start[devices[g] * per_device + j] == 1, place, first)

            @pl.when(owned[g][j] == 1)
            def _():
                code = g * pair + place
                out[spot.slot + code] = base + place
                out[spot.live + code] = jnp.int32(1)
                out[spot.first + code] = first
                out[spot.code_of_slot + base + place] = code

            place = place + owned[g][j]
    mine = [owner[var * per_device + j] for j in range(per_device)]
    for j in range(per_device):
        gap = lax.rem(mine[j] - var + owners, owners)
        place = jnp.int32(0)
        for i in range(j):
            place = place + (mine[i] == mine[j]).astype(jnp.int32)
        code = (gap - 1) * pair + place
        out[spot.local + j] = code
        out[spot.unit + code] = jnp.int32(j)


def choose_body(spot, quarters, pair, table, inverses, *refs):
    where = indices()
    outs, arrived = refs[:quarters], refs[quarters]
    copies = []
    for k in range(quarters):
        for p in range(pair):
            slot = table[spot.slot + held_by(where[1] ^ k, where[0]) * pair + p]
            ready = arrived.at[k * pair + p]
            copies.append(pltpu.make_async_copy(inverses.at[slot], outs[k].at[p], ready))
            copies[-1].start()
    for copy in copies:
        copy.wait()


def states_body(spot, quarters, pair, momentum, table, now, before, *outs):
    where = indices()
    for k in range(quarters):
        for p in range(pair):
            code = held_by(where[1] ^ k, where[0]) * pair + p
            slot = table[spot.slot + code]
            live = table[spot.live + code] == 1
            held = jnp.where(live, now[slot], 0.0)
            point = held + momentum * (held - jnp.where(live, before[slot], 0.0))
            high = point.astype(HALF)
            outs[k][0, p] = high
            outs[k][1, p] = (point - high.astype(F32)).astype(HALF)
            outs[k][2, p] = held.astype(HALF)


def panels_body(spot, quarters, pair, most, table, *refs):
    where = indices()
    panels, outs = refs[:quarters], refs[quarters:]
    width = panels[0].shape[2] // most
    row = held_by(where[1], where[0]) * pair
    for p in range(pair):
        first = table[spot.first + row + p]
        live = table[spot.live + row + p] == 1
        for q in range(pair):
            same = (table[spot.first + row + q] == first) & (table[spot.live + row + q] == 1)
            part = jnp.clip(q - first, 0, most - 1)
            columns = pl.ds(pl.multiple_of(part * width, width), width)
            for k in range(quarters):
                block = panels[k][p, :, columns]
                outs[k][p, :, q * width : (q + 1) * width] = jnp.where(same & live, block, jnp.zeros_like(block))


def local_values_body(spot, pair, turned, table, *refs):
    where = indices()
    pieces, out, held = refs[:-2], refs[-2], refs[-1]
    for k, piece in enumerate(pieces):
        held[k] = piece[...]
    for u in range(out.shape[0]):
        code = table[spot.local + u]
        group = lax.div(code, pair)
        at = (held_by_seen(group, where[0]) ^ where[1]) if turned else group
        out[u] = held[at, lax.rem(code, pair)]


def place_values(quarters, where, pieces, values):
    units, quarter_rows = pieces[0].shape[:2]
    for k in range(quarters):
        for u in range(units):
            at = u * quarters * quarter_rows + (where[1] ^ k) * quarter_rows
            values[pl.ds(pl.multiple_of(at, quarter_rows), quarter_rows), :] = pieces[k][u]


def load_body(partner, dosage, out, arrived):
    where = indices()
    core, chip = lax.rem(where[0], CORES), lax.div(where[0], CORES)
    chips = arrived.shape[0]
    rows = out.shape[0] // chips
    copies = []
    for i in range(chips):
        at = pl.multiple_of(((chip ^ i) * CORES + (core ^ partner)) * rows, rows)
        copies.append(
            pltpu.make_async_copy(dosage.at[pl.ds(at, rows), :], out.at[pl.ds(i * rows, rows), :], arrived.at[i])
        )
        copies[-1].start()
    for copy in copies:
        copy.wait()


def predict_body(quarters, scale, blocks, *refs):
    where = indices()
    pieces, (out, values) = refs[:quarters], refs[quarters:]
    place_values(quarters, where, pieces, values)
    chips, rows = out.shape[:2]
    for i in range(chips):
        block = blocks[i * rows : (i + 1) * rows, :]
        out[i] = (jnp.dot(block, values[...], preferred_element_type=F32) * scale).astype(out.dtype)


def turned_rows(pieces, residual):
    rows = pieces[0].shape[0]
    for i, piece in enumerate(pieces):
        residual[i * rows : (i + 1) * rows, :] = piece[...]
    return residual[...].T


def first_gradient_body(side, *refs):
    pieces, (out, residual) = refs[:-2], refs[-2:]
    turned = turned_rows(pieces, residual)
    width = out.shape[2]
    for u in range(out.shape[0]):
        out[u] = jnp.dot(turned, side[:, u * width : (u + 1) * width], preferred_element_type=F32)


def gradient_body(quarters, scale, side, started, *refs):
    where = indices()
    pieces, outs = refs[: -quarters - 2], refs[-quarters - 2 : -2]
    residual, total = refs[-2:]
    turned = turned_rows(pieces, residual)
    width = started.shape[2]
    quarter_rows = width // quarters
    for u in range(started.shape[0]):
        product = jnp.dot(turned, side[:, u * width : (u + 1) * width], preferred_element_type=F32)
        total[u] = (started[u] + product).T * scale
        for k in range(quarters):
            at = pl.multiple_of((where[1] ^ k) * quarter_rows, quarter_rows)
            outs[k][u] = total[u, pl.ds(at, quarter_rows), :].astype(outs[k].dtype)


def leave_body(spot, quarters, pair, table, *refs):
    where = indices()
    sums, outs = refs[:quarters], refs[quarters:]
    for k in range(quarters):
        for p in range(pair):
            unit = table[spot.unit + held_by_seen(where[1] ^ k, where[0]) * pair + p]
            at = jnp.maximum(unit, 0)
            total = sums[0][at]
            for j in range(1, quarters):
                total = total + sums[j][at].astype(F32)
            outs[k][p] = jnp.where(unit >= 0, total, 0.0).astype(HALF)


def update_body(quarters, momentum, penalty, *refs):
    where = indices()
    last = momentum is None
    panels, pieces, states = refs[:quarters], refs[quarters : 2 * quarters], refs[2 * quarters : 3 * quarters]
    outs, gradient = refs[3 * quarters : -1], refs[-1]
    pair, quarter_rows = pieces[0].shape[:2]
    for k in range(quarters):
        for p in range(pair):
            at = p * quarters * quarter_rows + (where[1] ^ k) * quarter_rows
            gradient[pl.ds(pl.multiple_of(at, quarter_rows), quarter_rows), :] = pieces[k][p]
    for k in range(quarters):
        panel = panels[k][...].reshape(pair * quarter_rows, -1)
        direction = jnp.dot(panel, gradient[...], preferred_element_type=F32)
        direction = direction.reshape(pair, quarter_rows, -1)
        if last:
            point = states[k][...]
        else:
            point = states[k][0].astype(F32) + states[k][1].astype(F32)
            now = states[k][2].astype(F32)
        stepped = point - direction
        size = jnp.maximum(jnp.abs(stepped) - penalty[...], 0.0)
        updated = jnp.where(stepped > 0, size, jnp.where(stepped < 0, -size, 0.0))
        if last:
            outs[k][...] = updated.astype(outs[k].dtype)
        else:
            following = updated + momentum * (updated - now)
            outs[k][...] = following
            outs[quarters + k][...] = following.astype(HALF)


def finish_body(spot, pair, table, *refs):
    where = indices()
    pieces, out, held = refs[:-2], refs[-2], refs[-1]
    for k, piece in enumerate(pieces):
        held[k] = piece[...].astype(F32)
    for slot in range(out.shape[0]):
        code = table[spot.code_of_slot + slot]
        known = jnp.maximum(code, 0)
        block = held[held_by(lax.div(known, pair), where[0]) ^ where[1], lax.rem(known, pair)]
        out[slot] = jnp.where(code >= 0, block, 0.0)


def steps(dosage, traits, coef_now, coef_prev, block_inverse, penalty, block_start, unit_owner):
    owners = lax.axis_size("var")
    quarters = lax.axis_size("samp")
    capacity, quarter_rows, right_cols = coef_now.shape
    block_most, unit_rows = block_inverse.shape[2:]
    per_device = dosage.shape[1] // unit_rows
    pair = min(block_most, per_device)
    reach = capacity // pair
    assert reach == quarters and owners % CORES == 0 and owners & (owners - 1) == 0
    chips = owners // CORES
    rows = dosage.shape[0] // owners
    codes = reach * pair
    inv_scale = 1.0 / math.sqrt(dosage.shape[1] * owners)
    grad_scale = 0.5 / math.sqrt(dosage.shape[0] * quarters)
    spot = Layout(codes, capacity, per_device)
    ranks = range(quarters)
    piece = (pair, quarter_rows, right_cols)
    share = (per_device, quarter_rows, right_cols)

    table, *sent = pl.pallas_call(
        functools.partial(begin_body, spot, owners, reach, pair, per_device, MOMENTA[0]),
        name="begin",
        in_specs=[SMEM] * 2 + [FAR] * 2,
        out_specs=[SMEM] + [VMEM] * reach,
        out_shape=[like((spot.size,), jnp.int32)] + [like(piece, HALF)] * reach,
        scratch_shapes=[pltpu.VMEM(coef_now.shape, F32)] * 2 + [pltpu.SemaphoreType.DMA((2,))],
        compiler_params=pltpu.CompilerParams(vmem_limit_bytes=60 * MIB),
    )(block_start, unit_owner, coef_now, coef_prev)
    arrived = [shifted(sent[g], "var", -g - 1) for g in range(reach)]
    chosen = local(
        functools.partial(choose_body, spot, quarters, pair),
        [table], [block_inverse], [like((pair, *block_inverse.shape[1:]), HALF)] * quarters,
        [pltpu.SemaphoreType.DMA((codes,))], limit=LARGE_CHOOSE, far=1,
    )
    block = like((chips * rows, dosage.shape[1]), HALF)
    later = lax.optimization_barrier((chosen[0], dosage))[1]
    given_rows = local(
        functools.partial(load_body, 1), [], [later], block,
        [pltpu.SemaphoreType.DMA((chips,))], limit=LARGE_FIRST, far=1,
    )
    arrived, chosen, given_rows = lax.optimization_barrier((arrived, chosen, given_rows))
    chosen = [chosen[0]] + [crossed(chosen[k], "samp", k) for k in ranks[1:]]
    penalty = penalty.reshape(1, 1, right_cols)

    for step in range(len(MOMENTA)):
        own = local(
            functools.partial(local_values_body, spot, pair, step > 0),
            [table], arrived, like(share, HALF),
            [pltpu.VMEM((reach, *piece), HALF)],
        )
        pieces = [own] + [crossed(own, "samp", k) for k in ranks[1:]]
        if step == 0:
            later = lax.optimization_barrier((own, dosage))[1]
            kept_rows = local(
                functools.partial(load_body, 0), [], [later], block,
                [pltpu.SemaphoreType.DMA((chips,))], limit=LARGE, far=1,
            )
            pieces, kept_rows = lax.optimization_barrier((pieces, kept_rows))
        buffers = [pltpu.VMEM((dosage.shape[1], right_cols), HALF)]
        flops = dosage.shape[0] * dosage.shape[1] * right_cols
        given, kept = (
            local(
                functools.partial(predict_body, quarters, inv_scale),
                [], [side, *pieces], like((chips, rows, right_cols), kind), buffers, limit=8, flops=flops,
            )
            for side, kind in ((given_rows, HALF), (kept_rows, F32))
        )
        given = crossed(given, "var", 1)
        both = kept + given.astype(F32)
        total = both[0]
        for part in fan(over_chips, both.astype(HALF), range(1, chips)):
            total = total + part.astype(F32)
        residual_b = (total - traits).astype(HALF)
        mine = [residual_b] + fan(over_chips, [residual_b] * chips, range(1, chips))
        others = [crossed(block, "var", 1) for block in mine]
        flops = dosage.shape[0] * dosage.shape[1] * right_cols
        stacked = pltpu.VMEM((chips * rows, right_cols), HALF)
        started = local(
            first_gradient_body, [], [kept_rows, *mine],
            like((per_device, right_cols, unit_rows), F32), [stacked], limit=8, flops=flops,
        )
        sums = local(
            functools.partial(gradient_body, quarters, grad_scale),
            [], [given_rows, started, *others],
            [like(share, F32 if k == 0 else HALF) for k in ranks],
            [stacked, pltpu.VMEM((per_device, unit_rows, right_cols), F32)], limit=10, flops=flops,
        )
        if step == len(MOMENTA) - 1:
            residual = lax.optimization_barrier((sums[0], total))[1] - traits
        summed = sums[0]
        sums = [summed] + fan(over_samp, sums, ranks[1:])
        if step == 0:
            held = lax.optimization_barrier((summed, coef_now, coef_prev))[1:]
            states = local(
                functools.partial(states_body, spot, quarters, pair, MOMENTA[0]),
                [table], list(held), [like((3, *piece), HALF)] * quarters,
            )
            states = [states[0]] + [crossed(states[k], "samp", k) for k in ranks[1:]]
        leaving = local(
            functools.partial(leave_body, spot, quarters, pair),
            [table], sums, [like(piece, HALF)] * quarters,
        )
        landed = [to_owners(leaving[k], k) for k in ranks]
        if step == 0:
            chosen = lax.optimization_barrier((leaving, chosen))[1]
            panels = local(
                functools.partial(panels_body, spot, quarters, pair, block_most),
                [table],
                [part.reshape(pair, quarter_rows, block_most * unit_rows) for part in chosen],
                [like((pair, quarter_rows, block_most * unit_rows), HALF)] * quarters, limit=10,
            )
        last = step == len(MOMENTA) - 1
        if last:
            outs = [like(piece, F32 if k == 0 else HALF) for k in ranks]
        else:
            outs = [like(piece, F32)] * quarters + [like(piece, HALF)] * quarters
        result = local(
            functools.partial(update_body, quarters, None if last else MOMENTA[step + 1]),
            [], [penalty, *panels, *landed, *states], outs,
            [pltpu.VMEM((pair * unit_rows, right_cols), HALF)], limit=12,
            flops=2 * (pair * unit_rows) ** 2 * right_cols,
        )
        states = list(result[:quarters])
        if not last:
            arrived = fan(to_variants, result[quarters:], ranks)
    states = [states[0]] + fan(over_samp, states, ranks[1:])
    current = local(
        functools.partial(finish_body, spot, pair),
        [table], states, like((capacity, quarter_rows, right_cols), F32),
        [pltpu.VMEM((quarters, *piece), F32)],
    )
    return (current, residual)


def solution(mesh):
    placed = (
        P("samp", "var"),
        P(("samp", "var"), None),
        P("var", "samp", None),
        P("var", "samp", None),
        P("var", "samp", None, None),
        P(),
        P(),
        P(),
    )
    return jax.shard_map(
        steps,
        mesh=mesh,
        in_specs=placed,
        out_specs=(P("var", "samp", None), P(("samp", "var"), None)),
        check_vma=False,
    )
```

```python
import functools
import math

import jax
import jax.numpy as jnp
from jax import lax
from jax.experimental import pallas as pl
from jax.experimental.pallas import tpu as pltpu
from jax.sharding import PartitionSpec as P


MOMENTA = (0.4, 0.55)
CORES = 2
MIB = 1 << 20
LARGE = 45
LARGE_FIRST = 46
LARGE_CHOOSE = 57


SMEM = pl.BlockSpec(memory_space=pltpu.SMEM)
VMEM = pl.BlockSpec(memory_space=pltpu.VMEM)
FAR = pl.BlockSpec(memory_space=pl.ANY)
F32, HALF = jnp.float32, jnp.bfloat16


def like(shape, dtype):
    return jax.ShapeDtypeStruct(shape, dtype)


def local(body, scalars, arrays, outs, scratch=(), limit=8, flops=0, far=0):
    single = not isinstance(outs, list)
    moved = sum(math.prod(a.shape) * a.dtype.itemsize for a in [*arrays, *([outs] if single else outs)])
    return pl.pallas_call(
        body,
        in_specs=[SMEM] * len(scalars) + [FAR] * far + [VMEM] * (len(arrays) - far),
        out_specs=VMEM if single else [VMEM] * len(outs),
        out_shape=outs,
        scratch_shapes=list(scratch),
        compiler_params=pltpu.CompilerParams(vmem_limit_bytes=limit * MIB),
        cost_estimate=pl.CostEstimate(flops=flops, bytes_accessed=moved, transcendentals=0),
    )(*scalars, *arrays)


def indices():
    return [lax.axis_index(axis).astype(jnp.int32) for axis in ("var", "samp")]


def shifted(block, axis, distance):
    count = lax.axis_size(axis)
    return lax.ppermute(block, axis, [((i - distance) % count, i) for i in range(count)])


def crossed(block, axis, mask):
    count = lax.axis_size(axis)
    return lax.ppermute(block, axis, [(i, i ^ mask) for i in range(count)])


def held_by(group, owner):
    return group ^ (2 * (owner & 1))


def held_by_seen(rank, variant):
    return rank ^ (2 * ((variant + rank + 1) & 1))


def fan(send, blocks, ranks):
    sent = []
    for k in ranks:
        sent.append(send(blocks[k], k))
    return sent


def over_samp(block, mask):
    return crossed(block, "samp", mask)


def over_chips(block, mask):
    return crossed(block, "var", CORES * mask)


def to_owners(block, mask):
    quarters, owners = lax.axis_size("samp"), lax.axis_size("var")
    route = [
        (s * owners + v, (s ^ mask) * owners + (v + held_by_seen(s ^ mask, v) + 1) % owners)
        for s in range(quarters)
        for v in range(owners)
    ]
    return lax.ppermute(block, ("samp", "var"), route)


def to_variants(block, mask):
    quarters, owners = lax.axis_size("samp"), lax.axis_size("var")
    route = [
        (s * owners + o, (s ^ mask) * owners + (o - held_by(s, o) - 1) % owners)
        for s in range(quarters)
        for o in range(owners)
    ]
    return lax.ppermute(block, ("samp", "var"), route)


class Layout:
    def __init__(self, codes, capacity, per_device):
        self.slot = 0
        self.live = self.slot + codes
        self.first = self.live + codes
        self.code_of_slot = self.first + codes
        self.local = self.code_of_slot + capacity
        self.unit = self.local + per_device
        self.size = self.unit + codes


def begin_body(spot, owners, reach, pair, per_device, momentum, start, owner, now, before, out, *refs):
    sent, (now_here, before_here, arrived) = refs[:reach], refs[reach:]
    copies = [
        pltpu.make_async_copy(now, now_here, arrived.at[0]),
        pltpu.make_async_copy(before, before_here, arrived.at[1]),
    ]
    for copy in copies:
        copy.start()
    tables_body(spot, owners, reach, pair, per_device, start, owner, out)
    for copy in copies:
        copy.wait()
    for g in range(reach):
        for p in range(pair):
            slot = out[spot.slot + g * pair + p]
            live = out[spot.live + g * pair + p]
            point = now_here[slot] + momentum * (now_here[slot] - before_here[slot])
            sent[g][p] = jnp.where(live == 1, point, 0.0).astype(HALF)


def tables_body(spot, owners, reach, pair, per_device, start, owner, out):
    where = indices()
    var = where[0]
    for i in range(spot.size):
        empty = spot.code_of_slot <= i < spot.local or i >= spot.unit
        out[i] = jnp.int32(-1 if empty else 0)
    devices = [lax.rem(var - gap + owners, owners) for gap in range(1, reach + 1)]
    owned = [
        [(owner[d * per_device + j] == var).astype(jnp.int32) for j in range(per_device)]
        for d in devices
    ]
    counts = [functools.reduce(lambda a, b: a + b, flags) for flags in owned]
    for g in range(reach):
        place = jnp.int32(0)
        first = jnp.int32(0)
        base = jnp.int32(0)
        for h in range(reach):
            if h != g:
                base = base + jnp.where(devices[h] < devices[g], counts[h], 0)
        for j in range(per_device):
            first = jnp.where(start[devices[g] * per_device + j] == 1, place, first)

            @pl.when(owned[g][j] == 1)
            def _():
                code = g * pair + place
                out[spot.slot + code] = base + place
                out[spot.live + code] = jnp.int32(1)
                out[spot.first + code] = first
                out[spot.code_of_slot + base + place] = code

            place = place + owned[g][j]
    mine = [owner[var * per_device + j] for j in range(per_device)]
    for j in range(per_device):
        gap = lax.rem(mine[j] - var + owners, owners)
        place = jnp.int32(0)
        for i in range(j):
            place = place + (mine[i] == mine[j]).astype(jnp.int32)
        code = (gap - 1) * pair + place
        out[spot.local + j] = code
        out[spot.unit + code] = jnp.int32(j)


def choose_body(spot, quarters, pair, table, inverses, *refs):
    where = indices()
    outs, arrived = refs[:quarters], refs[quarters]
    copies = []
    for k in range(quarters):
        for p in range(pair):
            slot = table[spot.slot + held_by(where[1] ^ k, where[0]) * pair + p]
            ready = arrived.at[k * pair + p]
            copies.append(pltpu.make_async_copy(inverses.at[slot], outs[k].at[p], ready))
            copies[-1].start()
    for copy in copies:
        copy.wait()


def states_body(spot, quarters, pair, momentum, table, now, before, *outs):
    where = indices()
    for k in range(quarters):
        for p in range(pair):
            code = held_by(where[1] ^ k, where[0]) * pair + p
            slot = table[spot.slot + code]
            live = table[spot.live + code] == 1
            held = jnp.where(live, now[slot], 0.0)
            point = held + momentum * (held - jnp.where(live, before[slot], 0.0))
            high = point.astype(HALF)
            outs[k][0, p] = high
            outs[k][1, p] = (point - high.astype(F32)).astype(HALF)
            outs[k][2, p] = held.astype(HALF)


def panels_body(spot, quarters, pair, most, table, *refs):
    where = indices()
    panels, outs = refs[:quarters], refs[quarters:]
    width = panels[0].shape[2] // most
    row = held_by(where[1], where[0]) * pair
    for p in range(pair):
        first = table[spot.first + row + p]
        live = table[spot.live + row + p] == 1
        for q in range(pair):
            same = (table[spot.first + row + q] == first) & (table[spot.live + row + q] == 1)
            part = jnp.clip(q - first, 0, most - 1)
            columns = pl.ds(pl.multiple_of(part * width, width), width)
            for k in range(quarters):
                block = panels[k][p, :, columns]
                outs[k][p, :, q * width : (q + 1) * width] = jnp.where(same & live, block, jnp.zeros_like(block))


def local_values_body(spot, pair, turned, table, *refs):
    where = indices()
    pieces, out, held = refs[:-2], refs[-2], refs[-1]
    for k, piece in enumerate(pieces):
        held[k] = piece[...]
    for u in range(out.shape[0]):
        code = table[spot.local + u]
        group = lax.div(code, pair)
        at = (held_by_seen(group, where[0]) ^ where[1]) if turned else group
        out[u] = held[at, lax.rem(code, pair)]


def place_values(quarters, where, pieces, values):
    units, quarter_rows = pieces[0].shape[:2]
    for k in range(quarters):
        for u in range(units):
            at = u * quarters * quarter_rows + (where[1] ^ k) * quarter_rows
            values[pl.ds(pl.multiple_of(at, quarter_rows), quarter_rows), :] = pieces[k][u]


def load_body(partner, dosage, out, arrived):
    for copy in started_load(partner, dosage, out, arrived):
        copy.wait()


def started_load(partner, dosage, out, arrived):
    where = indices()
    core, chip = lax.rem(where[0], CORES), lax.div(where[0], CORES)
    chips = arrived.shape[0]
    rows = out.shape[0] // chips
    copies = []
    for i in range(chips):
        at = pl.multiple_of(((chip ^ i) * CORES + (core ^ partner)) * rows, rows)
        copies.append(
            pltpu.make_async_copy(dosage.at[pl.ds(at, rows), :], out.at[pl.ds(i * rows, rows), :], arrived.at[i])
        )
        copies[-1].start()
    return copies


def loading_predict_body(quarters, scale, dosage, blocks, *refs):
    pieces, (out, kept, values, arrived) = refs[:quarters], refs[quarters:]
    copies = started_load(0, dosage, kept, arrived)
    predict_body(quarters, scale, blocks, *pieces, out, values)
    for copy in copies:
        copy.wait()


def predict_body(quarters, scale, blocks, *refs):
    where = indices()
    pieces, (out, values) = refs[:quarters], refs[quarters:]
    place_values(quarters, where, pieces, values)
    chips, rows = out.shape[:2]
    for i in range(chips):
        block = blocks[i * rows : (i + 1) * rows, :]
        out[i] = (jnp.dot(block, values[...], preferred_element_type=F32) * scale).astype(out.dtype)


def turned_rows(pieces, residual):
    rows = pieces[0].shape[0]
    for i, piece in enumerate(pieces):
        residual[i * rows : (i + 1) * rows, :] = piece[...]
    return residual[...].T


def first_gradient_body(side, *refs):
    pieces, (out, residual) = refs[:-2], refs[-2:]
    turned = turned_rows(pieces, residual)
    width = out.shape[2]
    for u in range(out.shape[0]):
        out[u] = jnp.dot(turned, side[:, u * width : (u + 1) * width], preferred_element_type=F32)


def gradient_body(quarters, scale, side, started, *refs):
    where = indices()
    pieces, outs = refs[: -quarters - 2], refs[-quarters - 2 : -2]
    residual, total = refs[-2:]
    turned = turned_rows(pieces, residual)
    width = started.shape[2]
    quarter_rows = width // quarters
    for u in range(started.shape[0]):
        product = jnp.dot(turned, side[:, u * width : (u + 1) * width], preferred_element_type=F32)
        total[u] = (started[u] + product).T * scale
        for k in range(quarters):
            at = pl.multiple_of((where[1] ^ k) * quarter_rows, quarter_rows)
            outs[k][u] = total[u, pl.ds(at, quarter_rows), :].astype(outs[k].dtype)


def leave_body(spot, quarters, pair, table, *refs):
    where = indices()
    sums, outs = refs[:quarters], refs[quarters:]
    for k in range(quarters):
        for p in range(pair):
            unit = table[spot.unit + held_by_seen(where[1] ^ k, where[0]) * pair + p]
            at = jnp.maximum(unit, 0)
            total = sums[0][at]
            for j in range(1, quarters):
                total = total + sums[j][at].astype(F32)
            outs[k][p] = jnp.where(unit >= 0, total, 0.0).astype(HALF)


def update_body(quarters, momentum, penalty, *refs):
    where = indices()
    last = momentum is None
    panels, pieces, states = refs[:quarters], refs[quarters : 2 * quarters], refs[2 * quarters : 3 * quarters]
    outs, gradient = refs[3 * quarters : -1], refs[-1]
    pair, quarter_rows = pieces[0].shape[:2]
    for k in range(quarters):
        for p in range(pair):
            at = p * quarters * quarter_rows + (where[1] ^ k) * quarter_rows
            gradient[pl.ds(pl.multiple_of(at, quarter_rows), quarter_rows), :] = pieces[k][p]
    for k in range(quarters):
        panel = panels[k][...].reshape(pair * quarter_rows, -1)
        direction = jnp.dot(panel, gradient[...], preferred_element_type=F32)
        direction = direction.reshape(pair, quarter_rows, -1)
        if last:
            point = states[k][...]
        else:
            point = states[k][0].astype(F32) + states[k][1].astype(F32)
            now = states[k][2].astype(F32)
        stepped = point - direction
        size = jnp.maximum(jnp.abs(stepped) - penalty[...], 0.0)
        updated = jnp.where(stepped > 0, size, jnp.where(stepped < 0, -size, 0.0))
        if last:
            outs[k][...] = updated.astype(outs[k].dtype)
        else:
            following = updated + momentum * (updated - now)
            outs[k][...] = following
            outs[quarters + k][...] = following.astype(HALF)


def finish_body(spot, pair, table, *refs):
    where = indices()
    pieces, out, held = refs[:-2], refs[-2], refs[-1]
    for k, piece in enumerate(pieces):
        held[k] = piece[...].astype(F32)
    for slot in range(out.shape[0]):
        code = table[spot.code_of_slot + slot]
        known = jnp.maximum(code, 0)
        block = held[held_by(lax.div(known, pair), where[0]) ^ where[1], lax.rem(known, pair)]
        out[slot] = jnp.where(code >= 0, block, 0.0)


def steps(dosage, traits, coef_now, coef_prev, block_inverse, penalty, block_start, unit_owner):
    owners = lax.axis_size("var")
    quarters = lax.axis_size("samp")
    capacity, quarter_rows, right_cols = coef_now.shape
    block_most, unit_rows = block_inverse.shape[2:]
    per_device = dosage.shape[1] // unit_rows
    pair = min(block_most, per_device)
    reach = capacity // pair
    assert reach == quarters and owners % CORES == 0 and owners & (owners - 1) == 0
    chips = owners // CORES
    rows = dosage.shape[0] // owners
    codes = reach * pair
    inv_scale = 1.0 / math.sqrt(dosage.shape[1] * owners)
    grad_scale = 0.5 / math.sqrt(dosage.shape[0] * quarters)
    spot = Layout(codes, capacity, per_device)
    ranks = range(quarters)
    piece = (pair, quarter_rows, right_cols)
    share = (per_device, quarter_rows, right_cols)

    table, *sent = pl.pallas_call(
        functools.partial(begin_body, spot, owners, reach, pair, per_device, MOMENTA[0]),
        name="begin",
        in_specs=[SMEM] * 2 + [FAR] * 2,
        out_specs=[SMEM] + [VMEM] * reach,
        out_shape=[like((spot.size,), jnp.int32)] + [like(piece, HALF)] * reach,
        scratch_shapes=[pltpu.VMEM(coef_now.shape, F32)] * 2 + [pltpu.SemaphoreType.DMA((2,))],
        compiler_params=pltpu.CompilerParams(vmem_limit_bytes=60 * MIB),
    )(block_start, unit_owner, coef_now, coef_prev)
    arrived = [shifted(sent[g], "var", -g - 1) for g in range(reach)]
    chosen = local(
        functools.partial(choose_body, spot, quarters, pair),
        [table], [block_inverse], [like((pair, *block_inverse.shape[1:]), HALF)] * quarters,
        [pltpu.SemaphoreType.DMA((codes,))], limit=LARGE_CHOOSE, far=1,
    )
    block = like((chips * rows, dosage.shape[1]), HALF)
    later = lax.optimization_barrier((chosen[0], dosage))[1]
    given_rows = local(
        functools.partial(load_body, 1), [], [later], block,
        [pltpu.SemaphoreType.DMA((chips,))], limit=LARGE_FIRST, far=1,
    )
    arrived, chosen, given_rows = lax.optimization_barrier((arrived, chosen, given_rows))
    chosen = [chosen[0]] + [crossed(chosen[k], "samp", k) for k in ranks[1:]]
    penalty = penalty.reshape(1, 1, right_cols)

    for step in range(len(MOMENTA)):
        own = local(
            functools.partial(local_values_body, spot, pair, step > 0),
            [table], arrived, like(share, HALF),
            [pltpu.VMEM((reach, *piece), HALF)],
        )
        pieces = [own] + [crossed(own, "samp", k) for k in ranks[1:]]
        buffers = [pltpu.VMEM((dosage.shape[1], right_cols), HALF)]
        flops = dosage.shape[0] * dosage.shape[1] * right_cols
        given, kept = (like((chips, rows, right_cols), kind) for kind in (HALF, F32))
        if step == 0:
            given, kept_rows = local(
                functools.partial(loading_predict_body, quarters, inv_scale),
                [], [dosage, given_rows, *pieces], [given, block],
                [*buffers, pltpu.SemaphoreType.DMA((chips,))], limit=LARGE, flops=flops, far=1,
            )
        else:
            given = local(
                functools.partial(predict_body, quarters, inv_scale),
                [], [given_rows, *pieces], given, buffers, limit=8, flops=flops,
            )
        kept = local(
            functools.partial(predict_body, quarters, inv_scale),
            [], [kept_rows, *pieces], kept, buffers, limit=8, flops=flops,
        )
        given = crossed(given, "var", 1)
        both = kept + given.astype(F32)
        total = both[0]
        for part in fan(over_chips, both.astype(HALF), range(1, chips)):
            total = total + part.astype(F32)
        residual_b = (total - traits).astype(HALF)
        mine = [residual_b] + fan(over_chips, [residual_b] * chips, range(1, chips))
        others = [crossed(block, "var", 1) for block in mine]
        flops = dosage.shape[0] * dosage.shape[1] * right_cols
        stacked = pltpu.VMEM((chips * rows, right_cols), HALF)
        started = local(
            first_gradient_body, [], [kept_rows, *mine],
            like((per_device, right_cols, unit_rows), F32), [stacked], limit=8, flops=flops,
        )
        sums = local(
            functools.partial(gradient_body, quarters, grad_scale),
            [], [given_rows, started, *others],
            [like(share, F32 if k == 0 else HALF) for k in ranks],
            [stacked, pltpu.VMEM((per_device, unit_rows, right_cols), F32)], limit=10, flops=flops,
        )
        if step == len(MOMENTA) - 1:
            residual = lax.optimization_barrier((sums[0], total))[1] - traits
        summed = sums[0]
        sums = [summed] + fan(over_samp, sums, ranks[1:])
        if step == 0:
            held = lax.optimization_barrier((summed, coef_now, coef_prev))[1:]
            states = local(
                functools.partial(states_body, spot, quarters, pair, MOMENTA[0]),
                [table], list(held), [like((3, *piece), HALF)] * quarters,
            )
            states = [states[0]] + [crossed(states[k], "samp", k) for k in ranks[1:]]
        leaving = local(
            functools.partial(leave_body, spot, quarters, pair),
            [table], sums, [like(piece, HALF)] * quarters,
        )
        landed = [to_owners(leaving[k], k) for k in ranks]
        if step == 0:
            chosen = lax.optimization_barrier((leaving, chosen))[1]
            panels = local(
                functools.partial(panels_body, spot, quarters, pair, block_most),
                [table],
                [part.reshape(pair, quarter_rows, block_most * unit_rows) for part in chosen],
                [like((pair, quarter_rows, block_most * unit_rows), HALF)] * quarters, limit=10,
            )
        last = step == len(MOMENTA) - 1
        if last:
            outs = [like(piece, F32 if k == 0 else HALF) for k in ranks]
        else:
            outs = [like(piece, F32)] * quarters + [like(piece, HALF)] * quarters
        result = local(
            functools.partial(update_body, quarters, None if last else MOMENTA[step + 1]),
            [], [penalty, *panels, *landed, *states], outs,
            [pltpu.VMEM((pair * unit_rows, right_cols), HALF)], limit=12,
            flops=2 * (pair * unit_rows) ** 2 * right_cols,
        )
        states = list(result[:quarters])
        if not last:
            arrived = fan(to_variants, result[quarters:], ranks)
    states = [states[0]] + fan(over_samp, states, ranks[1:])
    current = local(
        functools.partial(finish_body, spot, pair),
        [table], states, like((capacity, quarter_rows, right_cols), F32),
        [pltpu.VMEM((quarters, *piece), F32)],
    )
    return (current, residual)


def solution(mesh):
    placed = (
        P("samp", "var"),
        P(("samp", "var"), None),
        P("var", "samp", None),
        P("var", "samp", None),
        P("var", "samp", None, None),
        P(),
        P(),
        P(),
    )
    return jax.shard_map(
        steps,
        mesh=mesh,
        in_specs=placed,
        out_specs=(P("var", "samp", None), P(("samp", "var"), None)),
        check_vma=False,
    )
```
